32 devices in a mesh: dp: 2 (over x), seq: 4 (over z), tensor: 4 (over y, core).
Axes of the slice: x: 2, y: 2, z: 4, core: 2. Of those that a mesh axis runs over, the one named last changes fastest.
Arguments:
- hidden: float32 [4, 4096, 1024], P('dp', ('seq', 'tensor')), may hold values from -6 to 6
- out_cotangent: float32 [4, 4096, 1024], P('dp', ('seq', 'tensor')), may hold values from -6 to 6
- mixer_gain: float32 [1024], replicated, may hold values from 0.5 to 1.5
- input_weight: float32 [1024, 3, 1024], P(('dp', 'seq'), None, 'tensor'), may hold values from -0.1875 to 0.1875
- conv_weight: float32 [3, 1024], replicated, may hold values from -2 to 2
- output_weight: float32 [1024, 1024], P('tensor', ('dp', 'seq')), may hold values from -0.1875 to 0.1875
- feed_gain: float32 [1024], replicated, may hold values from 0.5 to 1.5
- gate_weight: float32 [1024, 4608], P(('dp', 'seq'), 'tensor'), may hold values from -0.1875 to 0.1875
- up_weight: float32 [1024, 4608], P(('dp', 'seq'), 'tensor'), may hold values from -0.1875 to 0.1875
- down_weight: float32 [4608, 1024], P('tensor', ('dp', 'seq')), may hold values from -0.09375 to 0.09375
- first_mixer_gain: float32 [1024], replicated, may hold values from -30 to 30
- first_input_weight: float32 [1024, 3, 1024], P(('dp', 'seq'), None, 'tensor'), may hold values from -30 to 30
- first_conv_weight: float32 [3, 1024], replicated, may hold values from -30 to 30
- first_output_weight: float32 [1024, 1024], P('tensor', ('dp', 'seq')), may hold values from -30 to 30
- first_feed_gain: float32 [1024], replicated, may hold values from -30 to 30
- first_gate_weight: float32 [1024, 4608], P(('dp', 'seq'), 'tensor'), may hold values from -30 to 30
- first_up_weight: float32 [1024, 4608], P(('dp', 'seq'), 'tensor'), may hold values from -30 to 30
- first_down_weight: float32 [4608, 1024], P('tensor', ('dp', 'seq')), may hold values from -30 to 30
- second_mixer_gain: float32 [1024], replicated, may hold values from 10 to 300
- second_input_weight: float32 [1024, 3, 1024], P(('dp', 'seq'), None, 'tensor'), may hold values from 10 to 300
- second_conv_weight: float32 [3, 1024], replicated, may hold values from 10 to 300
- second_output_weight: float32 [1024, 1024], P('tensor', ('dp', 'seq')), may hold values from 10 to 300
- second_feed_gain: float32 [1024], replicated, may hold values from 10 to 300
- second_gate_weight: float32 [1024, 4608], P(('dp', 'seq'), 'tensor'), may hold values from 10 to 300
- second_up_weight: float32 [1024, 4608], P(('dp', 'seq'), 'tensor'), may hold values from 10 to 300
- second_down_weight: float32 [4608, 1024], P('tensor', ('dp', 'seq')), may hold values from 10 to 300
Outputs:
- block_output: float32 [4, 4096, 1024], P('dp', ('seq', 'tensor'))
- hidden_grad: float32 [4, 4096, 1024], P('dp', ('seq', 'tensor'))
- grad_mixer_gain: float32 [1024], replicated
- grad_input_weight: float32 [1024, 3, 1024], P(('dp', 'seq'), None, 'tensor')
- grad_conv_weight: float32 [3, 1024], replicated
- grad_output_weight: float32 [1024, 1024], P('tensor', ('dp', 'seq'))
- grad_feed_gain: float32 [1024], replicated
- grad_gate_weight: float32 [1024, 4608], P(('dp', 'seq'), 'tensor')
- grad_up_weight: float32 [1024, 4608], P(('dp', 'seq'), 'tensor')
- grad_down_weight: float32 [4608, 1024], P('tensor', ('dp', 'seq'))
- new_mixer_gain: float32 [1024], replicated
- new_input_weight: float32 [1024, 3, 1024], P(('dp', 'seq'), None, 'tensor')
- new_conv_weight: float32 [3, 1024], replicated
- new_output_weight: float32 [1024, 1024], P('tensor', ('dp', 'seq'))
- new_feed_gain: float32 [1024], replicated
- new_gate_weight: float32 [1024, 4608], P(('dp', 'seq'), 'tensor')
- new_up_weight: float32 [1024, 4608], P(('dp', 'seq'), 'tensor')
- new_down_weight: float32 [4608, 1024], P('tensor', ('dp', 'seq'))
- new_first_mixer_gain: float32 [1024], replicated
- new_first_input_weight: float32 [1024, 3, 1024], P(('dp', 'seq'), None, 'tensor')
- new_first_conv_weight: float32 [3, 1024], replicated
- new_first_output_weight: float32 [1024, 1024], P('tensor', ('dp', 'seq'))
- new_first_feed_gain: float32 [1024], replicated
- new_first_gate_weight: float32 [1024, 4608], P(('dp', 'seq'), 'tensor')
- new_first_up_weight: float32 [1024, 4608], P(('dp', 'seq'), 'tensor')
- new_first_down_weight: float32 [4608, 1024], P('tensor', ('dp', 'seq'))
- new_second_mixer_gain: float32 [1024], replicated
- new_second_input_weight: float32 [1024, 3, 1024], P(('dp', 'seq'), None, 'tensor')
- new_second_conv_weight: float32 [3, 1024], replicated
- new_second_output_weight: float32 [1024, 1024], P('tensor', ('dp', 'seq'))
- new_second_feed_gain: float32 [1024], replicated
- new_second_gate_weight: float32 [1024, 4608], P(('dp', 'seq'), 'tensor')
- new_second_up_weight: float32 [1024, 4608], P(('dp', 'seq'), 'tensor')
- new_second_down_weight: float32 [4608, 1024], P('tensor', ('dp', 'seq'))
The draws below stay inside these ranges and needn't reach their ends.
All inputs are finite; a program needn't handle non-finite values.
Results may differ from the reference program's by a relative error of at most 0.025.
Values may be sent and summed in bfloat16 or wider, within the bound.
No kernel may reach another device: no remote copies, remote signals or barrier semaphores. Data moves between devices by JAX's collectives and lax.ppermute only.
A program may use at most 192 MiB of HBM per device.

```python
import math
import jax
import jax.numpy as jnp
from jax import lax

D = 1024
FF = 4608
LENGTH = 4096
SEQS = 2
STEP = 3
BATCH = 4
TOK_DEV = 1024
N_DP = 2
N_SEQ = 4
N_TENSOR = 4


def block_levels(own_key, dims, shards, low, top_value):
    level = 1.0
    for position, parts in shards:
        draws = jax.random.uniform(jax.random.fold_in(jax.random.fold_in(own_key, 6), position), (parts,), jnp.float32, low / len(shards), top_value / len(shards))
        level = level * jnp.repeat(jnp.exp(draws), dims[position] // parts).reshape((-1,) + (1,) * (len(dims) - 1 - position))
    return level


def centred(key, shape, spread, limit, cuts=(), kind=jnp.bfloat16):
    gain = block_levels(key, shape, cuts, -0.22, 0.18) if cuts else 1.0
    drawn = jax.random.normal(key, shape, jnp.float32) * spread * gain
    return jnp.minimum(jnp.maximum(drawn, -limit), limit).astype(kind)


def setup_inputs(seed: int = 0) -> dict:
    key_of = jax.random.split(jax.random.key(seed), 27)
    hidden = centred(key_of[0], (BATCH, LENGTH, D), 1.0, 6.0, ((0, 2), (1, 16)), jnp.float32)
    out_cotangent = centred(key_of[1], (BATCH, LENGTH, D), 1.0, 6.0, ((0, 2), (1, 16)), jnp.float32)
    mixer_gain = jnp.clip(1.0 + 0.1 * jax.random.normal(key_of[2], (D,), jnp.float32), 0.5, 1.5)
    input_weight = centred(key_of[3], (D, 3, D), D ** -0.5, 0.1875, ((0, 8), (2, 4)), jnp.float32)
    conv_weight = centred(key_of[4], (3, D), 0.5, 2.0, (), jnp.float32)
    output_weight = centred(key_of[5], (D, D), D ** -0.5, 0.1875, ((0, 4), (1, 8)), jnp.float32)
    feed_gain = jnp.clip(1.0 + 0.1 * jax.random.normal(key_of[6], (D,), jnp.float32), 0.5, 1.5)
    gate_weight = centred(key_of[7], (D, FF), D ** -0.5, 0.1875, ((0, 8), (1, 4)), jnp.float32)
    up_weight = centred(key_of[8], (D, FF), D ** -0.5, 0.1875, ((0, 8), (1, 4)), jnp.float32)
    down_weight = centred(key_of[9], (FF, D), FF ** -0.5, 0.09375, ((0, 4), (1, 8)), jnp.float32)
    first_mixer_gain = centred(key_of[10], (D,), 5.0, 30.0, (), jnp.float32)
    first_input_weight = centred(key_of[11], (D, 3, D), 5.0, 30.0, ((0, 8), (2, 4)), jnp.float32)
    first_conv_weight = centred(key_of[12], (3, D), 5.0, 30.0, (), jnp.float32)
    first_output_weight = centred(key_of[13], (D, D), 5.0, 30.0, ((0, 4), (1, 8)), jnp.float32)
    first_feed_gain = centred(key_of[14], (D,), 5.0, 30.0, (), jnp.float32)
    first_gate_weight = centred(key_of[15], (D, FF), 5.0, 30.0, ((0, 8), (1, 4)), jnp.float32)
    first_up_weight = centred(key_of[16], (D, FF), 5.0, 30.0, ((0, 8), (1, 4)), jnp.float32)
    first_down_weight = centred(key_of[17], (FF, D), 5.0, 30.0, ((0, 4), (1, 8)), jnp.float32)
    second_mixer_gain = jnp.clip(jnp.exp(jax.random.uniform(key_of[18], (D,), jnp.float32, math.log(10.0), math.log(300.0))), 10.0, 300.0)
    second_input_weight = jnp.clip(jnp.exp(math.log(300.0) - 3.4011974 * jax.random.uniform(key_of[19], (D, 3, D), jnp.float32) ** block_levels(key_of[19], (D, 3, D), ((0, 8), (2, 4)), -0.2, 0.2)), 10.0, 300.0)
    second_conv_weight = jnp.clip(jnp.exp(jax.random.uniform(key_of[20], (3, D), jnp.float32, math.log(10.0), math.log(300.0))), 10.0, 300.0)
    second_output_weight = jnp.clip(jnp.exp(math.log(300.0) - 3.4011974 * jax.random.uniform(key_of[21], (D, D), jnp.float32) ** block_levels(key_of[21], (D, D), ((0, 4), (1, 8)), -0.2, 0.2)), 10.0, 300.0)
    second_feed_gain = jnp.clip(jnp.exp(jax.random.uniform(key_of[22], (D,), jnp.float32, math.log(10.0), math.log(300.0))), 10.0, 300.0)
    second_gate_weight = jnp.clip(jnp.exp(math.log(300.0) - 3.4011974 * jax.random.uniform(key_of[23], (D, FF), jnp.float32) ** block_levels(key_of[23], (D, FF), ((0, 8), (1, 4)), -0.2, 0.2)), 10.0, 300.0)
    second_up_weight = jnp.clip(jnp.exp(math.log(300.0) - 3.4011974 * jax.random.uniform(key_of[24], (D, FF), jnp.float32) ** block_levels(key_of[24], (D, FF), ((0, 8), (1, 4)), -0.2, 0.2)), 10.0, 300.0)
    second_down_weight = jnp.clip(jnp.exp(math.log(300.0) - 3.4011974 * jax.random.uniform(key_of[25], (FF, D), jnp.float32) ** block_levels(key_of[25], (FF, D), ((0, 4), (1, 8)), -0.2, 0.2)), 10.0, 300.0)
    return {"hidden": hidden, "out_cotangent": out_cotangent, "mixer_gain": mixer_gain, "input_weight": input_weight, "conv_weight": conv_weight, "output_weight": output_weight, "feed_gain": feed_gain, "gate_weight": gate_weight, "up_weight": up_weight, "down_weight": down_weight, "first_mixer_gain": first_mixer_gain, "first_input_weight": first_input_weight, "first_conv_weight": first_conv_weight, "first_output_weight": first_output_weight, "first_feed_gain": first_feed_gain, "first_gate_weight": first_gate_weight, "first_up_weight": first_up_weight, "first_down_weight": first_down_weight, "second_mixer_gain": second_mixer_gain, "second_input_weight": second_input_weight, "second_conv_weight": second_conv_weight, "second_output_weight": second_output_weight, "second_feed_gain": second_feed_gain, "second_gate_weight": second_gate_weight, "second_up_weight": second_up_weight, "second_down_weight": second_down_weight}


norm_eps = 1e-05
beta_one = 0.9
beta_two = 0.95
adam_eps = 1e-08
matrix_rate = 0.005
vector_rate = 0.05
decay_rate = 0.1

def widen(tensor_value):
    return lax.optimization_barrier(tensor_value.astype(jnp.bfloat16)).astype(jnp.float32)

def norm_forward(row_values, gain_vector):
    inverse = lax.rsqrt(lax.optimization_barrier(jnp.mean(row_values * row_values, axis=-1, keepdims=True)) + norm_eps)
    normed = row_values * inverse
    return (normed, inverse, normed * gain_vector)

def norm_backward(grad_rows, normed, inverse, gain_vector):
    scaled = grad_rows * gain_vector
    grad_input = inverse * (scaled - normed * lax.optimization_barrier(jnp.mean(scaled * normed, axis=-1, keepdims=True)))
    return (grad_input, lax.optimization_barrier(jnp.sum(grad_rows * normed, axis=(0, 1))))

def adamw(weight, gradient, first_moment, second_moment, step_rate, decay_factor):
    first_new = beta_one * first_moment + (1.0 - beta_one) * gradient
    second_new = beta_two * second_moment + (1.0 - beta_two) * gradient * gradient
    first_hat = first_new / (1.0 - beta_one ** STEP)
    second_hat = second_new / (1.0 - beta_two ** STEP)
    weight_new = weight - step_rate * (first_hat / (jnp.sqrt(second_hat) + adam_eps) + decay_factor * weight)
    return (weight_new, first_new, second_new)

def grouped(left_side, right_side, pattern):
    left_groups = left_side.reshape((left_side.shape[0], N_SEQ, TOK_DEV) + left_side.shape[2:])
    right_groups = right_side.reshape((right_side.shape[0], N_SEQ, TOK_DEV) + right_side.shape[2:])
    return lax.optimization_barrier(jnp.sum(widen(jnp.einsum(pattern, left_groups, right_groups)), axis=0))

def reference(hidden, out_cotangent, mixer_gain, input_weight, conv_weight, output_weight, feed_gain, gate_weight, up_weight, down_weight, first_mixer_gain, first_input_weight, first_conv_weight, first_output_weight, first_feed_gain, first_gate_weight, first_up_weight, first_down_weight, second_mixer_gain, second_input_weight, second_conv_weight, second_output_weight, second_feed_gain, second_gate_weight, second_up_weight, second_down_weight):
    channel_width = D // N_TENSOR
    unit_width = FF // N_TENSOR
    input_full = widen(input_weight)
    output_full = widen(output_weight)
    gate_full = widen(gate_weight)
    up_full = widen(up_weight)
    down_full = widen(down_weight)
    input_blocks = input_full.reshape(D, 3, N_TENSOR, channel_width)
    output_blocks = output_full.reshape(N_TENSOR, channel_width, D)
    gate_blocks = gate_full.reshape(D, N_TENSOR, unit_width)
    up_blocks = up_full.reshape(D, N_TENSOR, unit_width)
    down_blocks = down_full.reshape(N_TENSOR, unit_width, D)

    def one_block(running, inputs):
        row_values, cotangent = inputs
        seq_count = row_values.shape[0]
        seq_length = row_values.shape[1]
        normed_one, inverse_one, scaled_one = norm_forward(row_values, mixer_gain)
        mixer_rows = widen(scaled_one)
        projected = jnp.einsum('std,dke->stke', mixer_rows, input_full)
        part_b = projected[:, :, 0]
        part_c = projected[:, :, 1]
        part_x = projected[:, :, 2]
        gated_in = widen(part_b * part_x)
        padded = jnp.pad(gated_in, ((0, 0), (2, 0), (0, 0)))
        conv_out = conv_weight[0] * padded[:, :seq_length] + conv_weight[1] * padded[:, 1:seq_length + 1] + conv_weight[2] * padded[:, 2:]
        mixed_out = widen(part_c * conv_out)
        branch = lax.optimization_barrier(jnp.sum(widen(jnp.einsum('stjk,jke->stje', mixed_out.reshape(seq_count, seq_length, N_TENSOR, channel_width), output_blocks)), axis=2))
        middle = row_values + branch
        normed_two, inverse_two, scaled_two = norm_forward(middle, feed_gain)
        feed_rows = widen(scaled_two)
        gate_pre = jnp.einsum('std,df->stf', feed_rows, gate_full)
        up_pre = jnp.einsum('std,df->stf', feed_rows, up_full)
        sigmoid_gate = jax.nn.sigmoid(gate_pre)
        silu_gate = gate_pre * sigmoid_gate
        activated = widen(silu_gate * up_pre)
        feed_out = lax.optimization_barrier(jnp.sum(widen(jnp.einsum('stjf,jfe->stje', activated.reshape(seq_count, seq_length, N_TENSOR, unit_width), down_blocks)), axis=2))
        block_output = middle + feed_out
        out_rows = widen(cotangent)
        grad_act = jnp.einsum('ste,fe->stf', out_rows, down_full)
        grad_gate_pre = widen(grad_act * up_pre * sigmoid_gate * (1.0 + gate_pre * (1.0 - sigmoid_gate)))
        grad_up_pre = widen(grad_act * silu_gate)
        gate_split = grad_gate_pre.reshape(seq_count, seq_length, N_TENSOR, unit_width)
        up_split = grad_up_pre.reshape(seq_count, seq_length, N_TENSOR, unit_width)
        feed_back = lax.optimization_barrier(jnp.sum(widen(jnp.einsum('stjf,djf->stjd', gate_split, gate_blocks) + jnp.einsum('stjf,djf->stjd', up_split, up_blocks)), axis=2))
        grad_middle_norm, feed_gain_part = norm_backward(feed_back, normed_two, inverse_two, feed_gain)
        grad_middle = cotangent + grad_middle_norm
        middle_rows = widen(grad_middle)
        grad_mixed = jnp.einsum('ste,ke->stk', middle_rows, output_full)
        grad_c = grad_mixed * conv_out
        grad_conv_out = grad_mixed * part_c
        conv_part = jnp.stack([lax.optimization_barrier(jnp.sum(grad_conv_out * padded[:, offset:offset + seq_length], axis=(0, 1))) for offset in range(3)])
        conv_tail = jnp.pad(grad_conv_out, ((0, 0), (0, 2), (0, 0)))
        grad_gated = conv_weight[0] * conv_tail[:, 2:] + conv_weight[1] * conv_tail[:, 1:seq_length + 1] + conv_weight[2] * conv_tail[:, :seq_length]
        grad_projected = widen(jnp.stack((grad_gated * part_x, grad_c, grad_gated * part_b), axis=2))
        mixer_back = lax.optimization_barrier(jnp.sum(widen(jnp.einsum('stkjc,dkjc->stjd', grad_projected.reshape(seq_count, seq_length, 3, N_TENSOR, channel_width), input_blocks)), axis=2))
        grad_hidden_norm, mixer_gain_part = norm_backward(mixer_back, normed_one, inverse_one, mixer_gain)
        hidden_grad = grad_middle + grad_hidden_norm
        additions = (mixer_gain_part, grouped(mixer_rows, grad_projected, 'sctd,sctke->cdke'), conv_part, grouped(mixed_out, middle_rows, 'sctk,scte->cke'), feed_gain_part, grouped(feed_rows, grad_gate_pre, 'sctd,sctf->cdf'), grouped(feed_rows, grad_up_pre, 'sctd,sctf->cdf'), grouped(activated, out_rows, 'sctf,scte->cfe'))
        running = tuple((total + extra for total, extra in zip(running, additions)))
        return (running, (block_output, hidden_grad))
    start_sums = (jnp.zeros((D,), jnp.float32), jnp.zeros((D, 3, D), jnp.float32), jnp.zeros((3, D), jnp.float32), jnp.zeros((D, D), jnp.float32), jnp.zeros((D,), jnp.float32), jnp.zeros((D, FF), jnp.float32), jnp.zeros((D, FF), jnp.float32), jnp.zeros((FF, D), jnp.float32))
    stacked_rows = hidden.reshape(N_DP, SEQS, LENGTH, D)
    stacked_cot = out_cotangent.reshape(N_DP, SEQS, LENGTH, D)
    gradients, outputs = lax.scan(one_block, start_sums, (stacked_rows, stacked_cot))
    block_output = outputs[0].reshape(BATCH, LENGTH, D)
    hidden_grad = outputs[1].reshape(BATCH, LENGTH, D)
    weights = (mixer_gain, input_weight, conv_weight, output_weight, feed_gain, gate_weight, up_weight, down_weight)
    firsts = (first_mixer_gain, first_input_weight, first_conv_weight, first_output_weight, first_feed_gain, first_gate_weight, first_up_weight, first_down_weight)
    seconds = (second_mixer_gain, second_input_weight, second_conv_weight, second_output_weight, second_feed_gain, second_gate_weight, second_up_weight, second_down_weight)
    is_vector = (True, False, True, False, True, False, False, False)
    updated = []
    for weight, gradient, first_moment, second_moment, vector_flag in zip(weights, gradients, firsts, seconds, is_vector):
        if vector_flag:
            updated.append(adamw(weight, gradient, first_moment, second_moment, vector_rate, 0.0))
        else:
            updated.append(adamw(weight, gradient, first_moment, second_moment, matrix_rate, decay_rate))
    return (block_output, hidden_grad, gradients[0], gradients[1], gradients[2], gradients[3], gradients[4], gradients[5], gradients[6], gradients[7], updated[0][0], updated[1][0], updated[2][0], updated[3][0], updated[4][0], updated[5][0], updated[6][0], updated[7][0], updated[0][1], updated[1][1], updated[2][1], updated[3][1], updated[4][1], updated[5][1], updated[6][1], updated[7][1], updated[0][2], updated[1][2], updated[2][2], updated[3][2], updated[4][2], updated[5][2], updated[6][2], updated[7][2])
```

```python
import functools

import jax
import jax.numpy as jnp
from jax import lax
from jax.experimental import pallas as pl
from jax.experimental.pallas import tpu as pltpu
from jax.sharding import PartitionSpec as P


STEP = 3

norm_eps = 1e-05
beta_one = 0.9
beta_two = 0.95
adam_eps = 1e-08
matrix_rate = 0.005
vector_rate = 0.05
decay_rate = 0.1

half = jnp.bfloat16
full = jnp.float32
owners = ("dp", "seq")


def shifted(block, axis, distance):
    devices = range(lax.axis_size(axis))
    route = [(i - distance, i) for i in devices if i - distance in devices]
    return lax.ppermute(block, axis, route)


def swapped(block, axis, distance):
    return lax.ppermute(block, axis, [(i, i ^ distance) for i in range(lax.axis_size(axis))])


def bits_of(size):
    return [1 << b for b in range(size.bit_length() - 1)]


def gather_rows(block):
    chunks = {0: block}
    for distance in reversed(bits_of(lax.axis_size("tensor"))):
        for k in sorted(chunks):
            chunks[k ^ distance] = swapped(chunks[k], "tensor", distance)
    return [chunks[k] for k in sorted(chunks)]


def reduce_rows(partial_of):
    size = lax.axis_size("tensor")
    sums = {}
    for k in reversed(range(size)):
        sums[k] = partial_of(k)
    distances = bits_of(size)
    for distance in distances:
        for k in sorted(sums, reverse=True):
            if k & distance:
                arrived = swapped(sums.pop(k).astype(half), "tensor", distance)
                kept = sums[k ^ distance]
                if k == distance and distance == distances[-1]:
                    kept = lax.optimization_barrier(kept)
                sums[k ^ distance] = kept + arrived.astype(full)
    return sums[0]


def ring_of():
    rows, columns = lax.axis_size("dp"), lax.axis_size("seq")
    ring = []
    for r in range(rows):
        line = [r * columns + c for c in range(columns)]
        ring += line if r % 2 == 0 else line[::-1]
    return ring


def ring_neighbour(ring, offset):
    size = len(ring)
    table = [0] * size
    for place, index in enumerate(ring):
        table[index] = ring[(place + offset) % size]
    return jnp.array(table, jnp.int32)[lax.axis_index(owners)]


def ring_shift(block, ring, direction):
    size = len(ring)
    return lax.ppermute(
        block, owners, [(ring[p], ring[(p + direction) % size]) for p in range(size)]
    )


def ring_gather(block):
    ring = ring_of()
    size = len(ring)
    rows = block.shape[0]
    result = jnp.zeros((rows * size,) + block.shape[1:], block.dtype)

    def place(result, piece, offset):
        start = ring_neighbour(ring, offset) * rows
        return lax.dynamic_update_slice_in_dim(result, piece, start, 0)

    result = place(result, block, 0)
    forward = backward = block
    for hop in range(1, size // 2 + 1):
        forward = ring_shift(forward, ring, 1)
        result = place(result, forward, -hop)
        if hop <= (size - 1) // 2:
            backward = ring_shift(backward, ring, -1)
            result = place(result, backward, hop)
    return result


def ring_scatter(partial):
    ring = ring_of()
    size = len(ring)
    rows = partial.shape[0] // size

    def piece(offset):
        start = ring_neighbour(ring, offset) * rows
        return lax.dynamic_slice_in_dim(partial, start, rows, 0).astype(full)

    total = piece(0)
    for direction, reach in ((1, size // 2), (-1, (size - 1) // 2)):
        running = None
        for hop in range(reach, 0, -1):
            own = piece(direction * hop)
            running = own if running is None else own + running.astype(full)
            running = ring_shift(running.astype(half), ring, direction)
        if running is not None:
            total = total + running.astype(full)
    return total


def sum_everywhere(block):
    for axis in ("tensor", "dp", "seq"):
        for distance in bits_of(lax.axis_size(axis)):
            block = block + swapped(block, axis, distance)
    return block


def norm_forward(row_values, gain_vector):
    inverse = lax.rsqrt(jnp.mean(row_values * row_values, axis=-1, keepdims=True) + norm_eps)
    normed = row_values * inverse
    return (normed, inverse, normed * gain_vector)


def norm_backward(grad_rows, normed, inverse, gain_vector):
    scaled = grad_rows * gain_vector
    return inverse * (scaled - normed * jnp.mean(scaled * normed, axis=-1, keepdims=True))


def adamw(weight, gradient, first_moment, second_moment, step_rate, decay_factor):
    first_new = beta_one * first_moment + (1.0 - beta_one) * gradient
    second_new = beta_two * second_moment + (1.0 - beta_two) * gradient * gradient
    first_hat = first_new / (1.0 - beta_one**STEP)
    second_hat = second_new / (1.0 - beta_two**STEP)
    weight_new = weight - step_rate * (
        first_hat / (jnp.sqrt(second_hat) + adam_eps) + decay_factor * weight
    )
    return (weight_new, first_new, second_new)


def divisor_tile(extent, unit, most):
    best = extent
    for tile in range(unit, min(extent, most) + 1, unit):
        if extent % tile == 0:
            best = tile
    return best


def feed_kernel(m_ref, e_ref, g_ref, u_ref, d_ref, *rest):
    v_ref, dp_ref, du_ref = rest[-3:]
    rows = m_ref[...]
    gate_pre = jnp.dot(rows, g_ref[...], preferred_element_type=full)
    up_pre = jnp.dot(rows, u_ref[...], preferred_element_type=full)
    grad_act = jnp.dot(e_ref[...], d_ref[...], preferred_element_type=full)
    sigmoid_gate = jax.nn.sigmoid(gate_pre)
    silu_gate = gate_pre * sigmoid_gate
    v_ref[...] = (silu_gate * up_pre).astype(half)
    du_ref[...] = (grad_act * silu_gate).astype(half)
    dp_ref[...] = (
        grad_act * up_pre * sigmoid_gate * (1.0 + gate_pre * (1.0 - sigmoid_gate))
    ).astype(half)


def feed_core(m_rows, e_rows, gate_up, down, total_rows, first_row, held):
    count, width = m_rows.shape
    units = down.shape[1]
    tile = divisor_tile(count, 16, 512)
    unit_tile = divisor_tile(units, 128, 384)
    unit_steps = units // unit_tile
    base = first_row // tile
    row_spec = pl.BlockSpec((tile, width), lambda j, i: (i, 0))
    weight_spec = pl.BlockSpec((width, unit_tile), lambda j, i: (0, j))
    up_base = unit_steps
    gate, up = gate_up, gate_up
    if unit_tile % 128:
        gate, up, up_base = gate_up[:, :units], gate_up[:, units:], 0
    up_spec = pl.BlockSpec((width, unit_tile), lambda j, i: (0, up_base + j))
    out_spec = pl.BlockSpec((tile, unit_tile), lambda j, i: (base + i, j))
    out_type = jax.ShapeDtypeStruct((total_rows, units), half)
    operands = [m_rows, e_rows, gate, up, down]
    in_specs = [row_spec, row_spec, weight_spec, up_spec, weight_spec]
    aliases = {}
    if held is not None:
        operands += list(held)
        in_specs += [pl.BlockSpec(memory_space=pl.ANY)] * 3
        aliases = {5: 0, 6: 1, 7: 2}
    return pl.pallas_call(
        feed_kernel,
        out_shape=(out_type,) * 3,
        grid=(unit_steps, count // tile),
        in_specs=in_specs,
        out_specs=(out_spec,) * 3,
        input_output_aliases=aliases,
        cost_estimate=pl.CostEstimate(
            flops=6 * count * width * units,
            bytes_accessed=4 * count * width + 6 * width * units + 6 * count * units,
            transcendentals=count * units,
        ),
        compiler_params=pltpu.CompilerParams(vmem_limit_bytes=48 << 20),
        name="feed_core",
    )(*operands)


def on_device(*arguments):
    hidden, out_cotangent = arguments[:2]
    weights, firsts, seconds = (arguments[2 + 8 * i : 10 + 8 * i] for i in range(3))
    (
        mixer_gain,
        input_weight,
        conv_weight,
        output_weight,
        feed_gain,
        gate_weight,
        up_weight,
        down_weight,
    ) = weights
    parts = lax.axis_size("tensor")
    place = lax.axis_index("tensor")
    seqs, rows, width = hidden.shape
    owned = input_weight.shape[0]
    channels = input_weight.shape[2]
    units = gate_weight.shape[1]

    mixer_own = jnp.concatenate(
        (input_weight.reshape(owned, 3 * channels).astype(half), output_weight.T.astype(half)),
        axis=1,
    )
    gate_up_own = jnp.concatenate((gate_weight.astype(half), up_weight.astype(half)), axis=1)
    down_own = down_weight.T.astype(half)
    gate_up = lax.all_gather(gate_up_own, owners, axis=0, tiled=True)
    mixer_full = ring_gather(mixer_own)
    input_full = mixer_full[:, : 3 * channels]
    output_full = mixer_full[:, 3 * channels :]
    down_full = ring_gather(down_own)

    channel_start = place * channels
    taps = lax.dynamic_slice_in_dim(conv_weight, channel_start, channels, 1)
    normed_one, inverse_one, scaled_one = norm_forward(hidden, mixer_gain)
    mixer_rows = jnp.stack(gather_rows(scaled_one.astype(half)))
    out_chunks = gather_rows(out_cotangent.astype(half))
    projected = jnp.einsum("kstd,de->kste", mixer_rows, input_full, preferred_element_type=full)
    part_b = projected[..., :channels]
    part_c = projected[..., channels : 2 * channels]
    part_x = projected[..., 2 * channels :]
    gated_in = (part_b * part_x).astype(half)

    places = [place ^ k for k in range(parts)]

    def pick(pieces, wanted):
        chosen = jnp.zeros_like(pieces[0])
        for k in range(parts):
            chosen = jnp.where(places[k] == wanted, pieces[k], chosen)
        return chosen

    tails = [gated_in[k, :, rows - 2 :] for k in range(parts)]
    carried = shifted(pick(tails, parts - 1), "seq", 1)
    before = jnp.stack(
        [
            jnp.where(places[k] == 0, carried, pick(tails, places[k] - 1))
            for k in range(parts)
        ]
    )
    padded = jnp.concatenate((before, gated_in), axis=2).astype(full)
    conv_out = (
        taps[0] * padded[:, :, :rows]
        + taps[1] * padded[:, :, 1 : rows + 1]
        + taps[2] * padded[:, :, 2:]
    )
    mixed_out = (part_c * conv_out).astype(half)

    def narrow(pattern, left, right):
        return jnp.einsum(pattern, left, right, preferred_element_type=full)

    branch = reduce_rows(lambda k: narrow("stk,ek->ste", mixed_out[k], output_full))
    middle = hidden + branch

    normed_two, inverse_two, scaled_two = norm_forward(middle, feed_gain)
    feed_chunks = gather_rows(scaled_two.astype(half))
    chunk_rows = seqs * rows
    total_rows = parts * chunk_rows
    near = parts // 2
    held = None
    halves = []
    for first in (0, near):
        m_half = jnp.concatenate(feed_chunks[first : first + near], axis=0)
        e_half = jnp.concatenate(out_chunks[first : first + near], axis=0)
        m_half = m_half.reshape(near * chunk_rows, width)
        e_half = e_half.reshape(near * chunk_rows, width)
        halves.append((m_half, e_half))
        held = feed_core(
            m_half, e_half, gate_up, down_full, total_rows, first * chunk_rows, held
        )
    activated, grad_gate_pre, grad_up_pre = held
    feed_rows = jnp.concatenate([h[0] for h in halves], axis=0)
    out_rows = jnp.concatenate([h[1] for h in halves], axis=0)

    def chunk(array, k):
        return array[k * chunk_rows : (k + 1) * chunk_rows]

    def feed_back(k):
        product = narrow("tf,df->td", chunk(grad_gate_pre, k), gate_up[:, :units])
        product = product + narrow("tf,df->td", chunk(grad_up_pre, k), gate_up[:, units:])
        return product.reshape(seqs, rows, width)

    grad_scaled_two = reduce_rows(feed_back)
    feed_gain_part = jnp.sum(grad_scaled_two * normed_two, axis=(0, 1))
    grad_middle = out_cotangent + norm_backward(
        grad_scaled_two, normed_two, inverse_two, feed_gain
    )
    middle_rows = jnp.stack(gather_rows(grad_middle.astype(half)))

    grad_gate = narrow("td,tf->df", feed_rows, grad_gate_pre).astype(half)
    grad_up = narrow("td,tf->df", feed_rows, grad_up_pre).astype(half)
    grad_down = narrow("td,tf->df", out_rows, activated).astype(half)
    owned_gate_up = lax.psum_scatter(
        jnp.concatenate((grad_gate, grad_up), axis=1), owners, scatter_dimension=0, tiled=True
    ).astype(full)
    owned_down = ring_scatter(grad_down).T
    block_output = middle + reduce_rows(
        lambda k: narrow("tf,df->td", chunk(activated, k), down_full).reshape(seqs, rows, width)
    )

    grad_mixed = narrow("kstd,dc->kstc", middle_rows, output_full)
    grad_output = narrow("kstd,kstc->dc", middle_rows, mixed_out)
    grad_c = grad_mixed * conv_out
    grad_conv_out = grad_mixed * part_c
    conv_part = jnp.stack(
        [
            jnp.sum(grad_conv_out * padded[:, :, tap : tap + rows], axis=(0, 1, 2))
            for tap in range(3)
        ]
    )
    heads = [grad_conv_out[k, :, :2] for k in range(parts)]
    following = shifted(pick(heads, 0), "seq", -1)
    after = jnp.stack(
        [
            jnp.where(places[k] == parts - 1, following, pick(heads, places[k] + 1))
            for k in range(parts)
        ]
    )
    conv_tail = jnp.concatenate((grad_conv_out, after), axis=2)
    grad_gated = (
        taps[0] * conv_tail[:, :, 2:]
        + taps[1] * conv_tail[:, :, 1 : rows + 1]
        + taps[2] * conv_tail[:, :, :rows]
    )
    grad_projected = jnp.concatenate(
        (
            (grad_gated * part_x).astype(half),
            grad_c.astype(half),
            (grad_gated * part_b).astype(half),
        ),
        axis=-1,
    )
    grad_input = narrow("kstd,kste->de", mixer_rows, grad_projected)
    mixer_gain_part = jnp.sum(grad_input * input_full.astype(full), axis=1) / mixer_gain
    owned_mixer = ring_scatter(
        jnp.concatenate((grad_input.astype(half), grad_output.astype(half)), axis=1)
    )
    grad_scaled_one = reduce_rows(
        lambda k: narrow("ste,de->std", grad_projected[k], input_full)
    )
    hidden_grad = grad_middle + norm_backward(
        grad_scaled_one, normed_one, inverse_one, mixer_gain
    )

    conv_placed = lax.dynamic_update_slice_in_dim(
        jnp.zeros(conv_weight.shape, full), conv_part, channel_start, 1
    )
    vectors = sum_everywhere(
        jnp.concatenate((mixer_gain_part[None], feed_gain_part[None], conv_placed), axis=0)
    )
    gradients = (
        vectors[0],
        owned_mixer[:, : 3 * channels].reshape(owned, 3, channels),
        vectors[2:],
        owned_mixer[:, 3 * channels :].T,
        vectors[1],
        owned_gate_up[:, :units],
        owned_gate_up[:, units:],
        owned_down,
    )
    vector_flags = (True, False, True, False, True, False, False, False)
    updated = [
        adamw(
            weight,
            gradient,
            first,
            second,
            vector_rate if flag else matrix_rate,
            0.0 if flag else decay_rate,
        )
        for weight, gradient, first, second, flag in zip(
            weights, gradients, firsts, seconds, vector_flags
        )
    ]
    return (
        (block_output, hidden_grad)
        + gradients
        + tuple(u[0] for u in updated)
        + tuple(u[1] for u in updated)
        + tuple(u[2] for u in updated)
    )


def solution(mesh):
    row_spec = P("dp", ("seq", "tensor"), None)
    weight_specs = (
        P(),
        P(owners, None, "tensor"),
        P(),
        P("tensor", owners),
        P(),
        P(owners, "tensor"),
        P(owners, "tensor"),
        P("tensor", owners),
    )
    in_specs = (row_spec, row_spec) + weight_specs * 3
    out_specs = (row_spec, row_spec) + weight_specs * 4
    return jax.shard_map(
        on_device, mesh=mesh, in_specs=in_specs, out_specs=out_specs, check_vma=False
    )
```

```python
import functools

import jax
import jax.numpy as jnp
from jax import lax
from jax.experimental import pallas as pl
from jax.experimental.pallas import tpu as pltpu
from jax.sharding import PartitionSpec as P


STEP = 3

norm_eps = 1e-05
beta_one = 0.9
beta_two = 0.95
adam_eps = 1e-08
matrix_rate = 0.005
vector_rate = 0.05
decay_rate = 0.1

half = jnp.bfloat16
full = jnp.float32
owners = ("dp", "seq")


def shifted(block, axis, distance):
    devices = range(lax.axis_size(axis))
    route = [(i - distance, i) for i in devices if i - distance in devices]
    return lax.ppermute(block, axis, route)


def swapped(block, axis, distance):
    return lax.ppermute(block, axis, [(i, i ^ distance) for i in range(lax.axis_size(axis))])


def bits_of(size):
    return [1 << b for b in range(size.bit_length() - 1)]


def reversed_bits(index, size):
    return int(f"{index + size:b}"[:0:-1], 2) if size > 1 else 0


def gather_rows(block):
    stack = block[None]
    for distance in reversed(bits_of(lax.axis_size("tensor"))):
        stack = jnp.concatenate((stack, swapped(stack, "tensor", distance)))
    return stack


def gather_chunks(block):
    size = lax.axis_size("tensor")
    chunks = {0: block}
    for distance in reversed(bits_of(size)):
        for k in sorted(chunks):
            chunks[k ^ distance] = swapped(chunks[k], "tensor", distance)
    return [chunks[reversed_bits(p, size)] for p in range(size)]


def reduce_rows(partial_of, pieces=1):
    size = lax.axis_size("tensor")
    if size == 1:
        return partial_of(0, 1)[0]
    low = size // 2
    step = low // pieces
    arrived = {}
    for start in reversed(range(low, size, step)):
        sent = partial_of(start, start + step).astype(half)
        arrived[start - low] = swapped(sent, "tensor", 1).astype(full)
    sums = {}
    quarter = max(low // 2, 1)
    for start in reversed(range(0, low, quarter)):
        if step >= quarter:
            key = start - start % step
            piece = arrived[key][start - key : start - key + quarter]
        else:
            piece = jnp.concatenate([arrived[k] for k in range(start, start + quarter, step)])
        sums[start] = partial_of(start, start + quarter) + piece
    if low == 1:
        return sums[0][0]
    far, near = sums[quarter], sums[0]
    distance = 2
    while True:
        sent = far.astype(half)
        (near,) = lax.optimization_barrier((near,))
        near = near + swapped(sent, "tensor", distance).astype(full)
        if near.shape[0] == 1:
            return near[0]
        distance *= 2
        middle = near.shape[0] // 2
        far, near = near[middle:], near[:middle]


def ring_of():
    rows, columns = lax.axis_size("dp"), lax.axis_size("seq")
    ring = []
    for r in range(rows):
        line = [r * columns + c for c in range(columns)]
        ring += line if r % 2 == 0 else line[::-1]
    return ring


def ring_neighbour(ring, offset):
    size = len(ring)
    table = [0] * size
    for place, index in enumerate(ring):
        table[index] = ring[(place + offset) % size]
    return jnp.array(table, jnp.int32)[lax.axis_index(owners)]


def ring_shift(block, ring, direction):
    size = len(ring)
    return lax.ppermute(
        block, owners, [(ring[p], ring[(p + direction) % size]) for p in range(size)]
    )


def ring_gather(block):
    ring = ring_of()
    size = len(ring)
    rows = block.shape[0]
    result = jnp.zeros((rows * size,) + block.shape[1:], block.dtype)

    def place(result, piece, offset):
        start = ring_neighbour(ring, offset) * rows
        return lax.dynamic_update_slice_in_dim(result, piece, start, 0)

    result = place(result, block, 0)
    forward = backward = block
    for hop in range(1, size // 2 + 1):
        forward = ring_shift(forward, ring, 1)
        result = place(result, forward, -hop)
        if hop <= (size - 1) // 2:
            backward = ring_shift(backward, ring, -1)
            result = place(result, backward, hop)
    return result


def ring_scatter(partial):
    ring = ring_of()
    size = len(ring)
    rows = partial.shape[0] // size

    def piece(offset):
        start = ring_neighbour(ring, offset) * rows
        return lax.dynamic_slice_in_dim(partial, start, rows, 0).astype(full)

    total = piece(0)
    for direction, reach in ((1, size // 2), (-1, (size - 1) // 2)):
        running = None
        for hop in range(reach, 0, -1):
            own = piece(direction * hop)
            running = own if running is None else own + running.astype(full)
            running = ring_shift(running.astype(half), ring, direction)
        if running is not None:
            total = total + running.astype(full)
    return total


def sum_everywhere(block):
    for axis in ("tensor", "dp", "seq"):
        for distance in bits_of(lax.axis_size(axis)):
            block = block + swapped(block, axis, distance)
    return block


def norm_forward(row_values, gain_vector):
    inverse = lax.rsqrt(jnp.mean(row_values * row_values, axis=-1, keepdims=True) + norm_eps)
    normed = row_values * inverse
    return (normed, inverse, normed * gain_vector)


def norm_backward(grad_rows, normed, inverse, gain_vector):
    scaled = grad_rows * gain_vector
    return inverse * (scaled - normed * jnp.mean(scaled * normed, axis=-1, keepdims=True))


def adamw(weight, gradient, first_moment, second_moment, step_rate, decay_factor):
    first_new = beta_one * first_moment + (1.0 - beta_one) * gradient
    second_new = beta_two * second_moment + (1.0 - beta_two) * gradient * gradient
    first_hat = first_new / (1.0 - beta_one**STEP)
    second_hat = second_new / (1.0 - beta_two**STEP)
    weight_new = weight - step_rate * (
        first_hat / (jnp.sqrt(second_hat) + adam_eps) + decay_factor * weight
    )
    return (weight_new, first_new, second_new)


def divisor_tile(extent, unit, most):
    best = extent
    for tile in range(unit, min(extent, most) + 1, unit):
        if extent % tile == 0:
            best = tile
    return best


def feed_kernel(chunks, *refs):
    m_refs, (e_ref, w_ref, d_ref) = refs[:chunks], refs[chunks : chunks + 3]
    v_ref, p_ref = refs[-2:]
    unit_tile = d_ref.shape[1]
    for q in range(chunks):
        both = jnp.dot(m_refs[q][...], w_ref[...], preferred_element_type=full)
        grad_act = jnp.dot(e_ref[q, 0], d_ref[...], preferred_element_type=full)
        gate_pre, up_pre = both[:, :unit_tile], both[:, unit_tile:]
        sigmoid_gate = jax.nn.sigmoid(gate_pre)
        silu_gate = gate_pre * sigmoid_gate
        v_ref[q, 0] = (silu_gate * up_pre).astype(half)
        p_ref[q, 0, :, :unit_tile] = (
            grad_act * up_pre * sigmoid_gate * (1.0 + gate_pre * (1.0 - sigmoid_gate))
        ).astype(half)
        p_ref[q, 0, :, unit_tile:] = (grad_act * silu_gate).astype(half)


def feed_core(m_chunks, e_rows, feed_full, unit_tile, side, held):
    chunks = len(m_chunks)
    count, width = m_chunks[0].shape
    units = feed_full.shape[1] // 3
    steps = units // unit_tile
    down, down_base = feed_full, 2 * steps
    if unit_tile % 128:
        down, down_base = feed_full[:, 2 * units :], 0
    chunk_spec = pl.BlockSpec((count, width), lambda j: (0, 0))

    def row_spec(columns):
        return pl.BlockSpec((chunks, 1, count, columns), lambda j: (0, side, 0, j))

    operands = list(m_chunks) + [e_rows, feed_full, down]
    in_specs = [chunk_spec] * chunks + [
        pl.BlockSpec((chunks, 1, count, width), lambda j: (0, side, 0, 0)),
        pl.BlockSpec((width, 2 * unit_tile), lambda j: (0, j)),
        pl.BlockSpec((width, unit_tile), lambda j: (0, down_base + j)),
    ]
    aliases = {}
    if held is not None:
        aliases = {len(operands) + i: i for i in range(2)}
        operands += list(held)
        in_specs += [pl.BlockSpec(memory_space=pl.ANY)] * 2
    work = chunks * count
    return pl.pallas_call(
        functools.partial(feed_kernel, chunks),
        out_shape=tuple(
            jax.ShapeDtypeStruct((chunks, 2, count, c), half) for c in (units, 2 * units)
        ),
        grid=(steps,),
        in_specs=in_specs,
        out_specs=(row_spec(unit_tile), row_spec(2 * unit_tile)),
        input_output_aliases=aliases,
        cost_estimate=pl.CostEstimate(
            flops=6 * work * width * units,
            bytes_accessed=4 * work * width + 6 * width * units + 6 * work * units,
            transcendentals=work * units,
        ),
        compiler_params=pltpu.CompilerParams(vmem_limit_bytes=56 << 20),
        name="feed_core",
    )(*operands)


def interleave(gate, up, tile):
    pieces = []
    for start in range(0, gate.shape[1], tile):
        pieces += [gate[:, start : start + tile], up[:, start : start + tile]]
    return pieces


def separate(both, tile):
    pieces = [both[:, start : start + tile] for start in range(0, both.shape[1], tile)]
    return jnp.concatenate(pieces[::2], axis=1), jnp.concatenate(pieces[1::2], axis=1)


def on_device(*arguments):
    hidden, out_cotangent = arguments[:2]
    weights, firsts, seconds = (arguments[2 + 8 * i : 10 + 8 * i] for i in range(3))
    (
        mixer_gain,
        input_weight,
        conv_weight,
        output_weight,
        feed_gain,
        gate_weight,
        up_weight,
        down_weight,
    ) = weights
    parts = lax.axis_size("tensor")
    place = lax.axis_index("tensor")
    seqs, rows, width = hidden.shape
    owned = input_weight.shape[0]
    channels = input_weight.shape[2]
    units = gate_weight.shape[1]

    mixer_own = jnp.concatenate(
        (input_weight.reshape(owned, 3 * channels).astype(half), output_weight.T.astype(half)),
        axis=1,
    )
    unit_tile = divisor_tile(units, 128, 384)
    feed_own = jnp.concatenate(
        interleave(gate_weight.astype(half), up_weight.astype(half), unit_tile)
        + [down_weight.T.astype(half)],
        axis=1,
    )
    feed_full = lax.all_gather(feed_own, owners, axis=0, tiled=True)
    with jax.named_scope("mixer_ring"):
        mixer_full = ring_gather(mixer_own)
    input_full = mixer_full[:, : 3 * channels]
    output_full = mixer_full[:, 3 * channels :]

    channel_start = place * channels
    taps = lax.dynamic_slice_in_dim(conv_weight, channel_start, channels, 1)
    normed_one, inverse_one, scaled_one = norm_forward(hidden, mixer_gain)
    with jax.named_scope("gather_a"):
        mixer_rows = gather_rows(scaled_one.astype(half))
    with jax.named_scope("gather_e"):
        out_sent, mixer_rows_started = lax.optimization_barrier(
            (out_cotangent.astype(half), scaled_one.astype(half))
        )
        out_rows = gather_rows(out_sent)
    projected = jnp.einsum("kstd,de->kste", mixer_rows, input_full, preferred_element_type=full)
    part_b = projected[..., :channels]
    part_c = projected[..., channels : 2 * channels]
    part_x = projected[..., 2 * channels :]
    gated_in = (part_b * part_x).astype(half)

    places = [place ^ reversed_bits(p, parts) for p in range(parts)]

    def pick(pieces, wanted):
        chosen = jnp.zeros_like(pieces[0])
        for k in range(parts):
            chosen = jnp.where(places[k] == wanted, pieces[k], chosen)
        return chosen

    tails = [gated_in[k, :, rows - 2 :] for k in range(parts)]
    with jax.named_scope("halo_forward"):
        carried = shifted(pick(tails, parts - 1), "seq", 1)
    before = jnp.stack(
        [
            jnp.where(places[k] == 0, carried, pick(tails, places[k] - 1))
            for k in range(parts)
        ]
    )
    padded = jnp.concatenate((before, gated_in), axis=2).astype(full)
    conv_out = (
        taps[0] * padded[:, :, :rows]
        + taps[1] * padded[:, :, 1 : rows + 1]
        + taps[2] * padded[:, :, 2:]
    )
    mixed_out = (part_c * conv_out).astype(half)

    def narrow(pattern, left, right):
        return jnp.einsum(pattern, left, right, preferred_element_type=full)

    with jax.named_scope("reduce_o"):
        branch = reduce_rows(
            lambda low, high: narrow("kstc,dc->kstd", mixed_out[low:high], output_full)
        )
    middle = hidden + branch

    normed_two, inverse_two, scaled_two = norm_forward(middle, feed_gain)
    chunk_rows = seqs * rows
    with jax.named_scope("gather_m"):
        feed_chunks = gather_chunks(scaled_two.astype(half).reshape(chunk_rows, width))
    e_rows = out_rows.reshape(parts // 2, 2, chunk_rows, width)
    held = None
    for side in range(2):
        held = feed_core(feed_chunks[side::2], e_rows, feed_full, unit_tile, side, held)
    activated, grad_pre = (h.reshape((parts, chunk_rows, h.shape[-1])) for h in held)
    gate_up_full = feed_full[:, : 2 * units]
    down_full = feed_full[:, 2 * units :]
    feed_rows = jnp.stack(feed_chunks)

    def feed_back(low, high):
        product = narrow("ktf,df->ktd", grad_pre[low:high], gate_up_full)
        return product

    with jax.named_scope("reduce_dm"):
        grad_scaled_two = reduce_rows(feed_back, 2).reshape(seqs, rows, width)
    with jax.named_scope("weight_grads"):
        grad_gate_up = narrow("ktd,ktf->df", feed_rows, grad_pre).astype(half)
        grad_down = narrow(
            "ktd,ktf->df", out_rows.reshape(parts, chunk_rows, width), activated
        ).astype(half)
    grad_scaled_two, grad_gate_up, grad_down = lax.optimization_barrier(
        (grad_scaled_two, grad_gate_up, grad_down)
    )
    owned_gate_up = lax.psum_scatter(
        grad_gate_up, owners, scatter_dimension=0, tiled=True
    ).astype(full)
    feed_gain_part = jnp.sum(grad_scaled_two * normed_two, axis=(0, 1))
    grad_middle = out_cotangent + norm_backward(
        grad_scaled_two, normed_two, inverse_two, feed_gain
    )
    grad_middle_sent, activated = lax.optimization_barrier((grad_middle.astype(half), activated))
    with jax.named_scope("gather_dmid"):
        middle_rows = gather_rows(grad_middle_sent)
    with jax.named_scope("down_ring"):
        owned_down = ring_scatter(grad_down).T
    with jax.named_scope("reduce_f"):
        block_output = middle + reduce_rows(
            lambda low, high: narrow("ktf,df->ktd", activated[low:high], down_full)
        ).reshape(seqs, rows, width)

    grad_mixed = narrow("kstd,dc->kstc", middle_rows, output_full)
    grad_output = narrow("kstd,kstc->dc", middle_rows, mixed_out)
    grad_c = grad_mixed * conv_out
    grad_conv_out = grad_mixed * part_c
    conv_part = jnp.stack(
        [
            jnp.sum(grad_conv_out * padded[:, :, tap : tap + rows], axis=(0, 1, 2))
            for tap in range(3)
        ]
    )
    heads = [grad_conv_out[k, :, :2] for k in range(parts)]
    with jax.named_scope("halo_backward"):
        following = shifted(pick(heads, 0), "seq", -1)
    after = jnp.stack(
        [
            jnp.where(places[k] == parts - 1, following, pick(heads, places[k] + 1))
            for k in range(parts)
        ]
    )
    conv_tail = jnp.concatenate((grad_conv_out, after), axis=2)
    grad_gated = (
        taps[0] * conv_tail[:, :, 2:]
        + taps[1] * conv_tail[:, :, 1 : rows + 1]
        + taps[2] * conv_tail[:, :, :rows]
    )
    grad_projected = jnp.concatenate(
        (
            (grad_gated * part_x).astype(half),
            grad_c.astype(half),
            (grad_gated * part_b).astype(half),
        ),
        axis=-1,
    )
    grad_input = narrow("kstd,kste->de", mixer_rows, grad_projected).astype(half)
    grad_mixer = jnp.concatenate((grad_input, grad_output.astype(half)), axis=1)
    (grad_mixer,) = lax.optimization_barrier((grad_mixer,))
    mixer_gain_part = (
        jnp.sum(
            grad_mixer[:, : 3 * channels].astype(full) * input_full.astype(full), axis=1
        )
        / mixer_gain
    )
    with jax.named_scope("mixer_scatter"):
        owned_mixer = ring_scatter(grad_mixer)
    with jax.named_scope("reduce_da"):
        grad_scaled_one = reduce_rows(
            lambda low, high: narrow("kste,de->kstd", grad_projected[low:high], input_full)
        )
    hidden_grad = grad_middle + norm_backward(
        grad_scaled_one, normed_one, inverse_one, mixer_gain
    )

    conv_placed = lax.dynamic_update_slice_in_dim(
        jnp.zeros(conv_weight.shape, full), conv_part, channel_start, 1
    )
    with jax.named_scope("vectors"):
        vectors = sum_everywhere(
            jnp.concatenate((mixer_gain_part[None], feed_gain_part[None], conv_placed), axis=0)
        )
    owned_gate, owned_up = separate(owned_gate_up, unit_tile)
    gradients = (
        vectors[0],
        owned_mixer[:, : 3 * channels].reshape(owned, 3, channels),
        vectors[2:],
        owned_mixer[:, 3 * channels :].T,
        vectors[1],
        owned_gate,
        owned_up,
        owned_down,
    )
    vector_flags = (True, False, True, False, True, False, False, False)
    updated = [
        adamw(
            weight,
            gradient,
            first,
            second,
            vector_rate if flag else matrix_rate,
            0.0 if flag else decay_rate,
        )
        for weight, gradient, first, second, flag in zip(
            weights, gradients, firsts, seconds, vector_flags
        )
    ]
    return (
        (block_output, hidden_grad)
        + gradients
        + tuple(u[0] for u in updated)
        + tuple(u[1] for u in updated)
        + tuple(u[2] for u in updated)
    )


def solution(mesh):
    row_spec = P("dp", ("seq", "tensor"), None)
    weight_specs = (
        P(),
        P(owners, None, "tensor"),
        P(),
        P("tensor", owners),
        P(),
        P(owners, "tensor"),
        P(owners, "tensor"),
        P("tensor", owners),
    )
    in_specs = (row_spec, row_spec) + weight_specs * 3
    out_specs = (row_spec, row_spec) + weight_specs * 4
    return jax.shard_map(
        on_device, mesh=mesh, in_specs=in_specs, out_specs=out_specs, check_vma=False
    )
```

```python
import functools

import jax
import jax.numpy as jnp
from jax import lax
from jax.experimental import pallas as pl
from jax.experimental.pallas import tpu as pltpu
from jax.sharding import PartitionSpec as P


STEP = 3

norm_eps = 1e-05
beta_one = 0.9
beta_two = 0.95
adam_eps = 1e-08
matrix_rate = 0.005
vector_rate = 0.05
decay_rate = 0.1

half = jnp.bfloat16
full = jnp.float32
owners = ("dp", "seq")


def shifted(block, axis, distance):
    devices = range(lax.axis_size(axis))
    route = [(i - distance, i) for i in devices if i - distance in devices]
    return lax.ppermute(block, axis, route)


def swapped(block, axis, distance):
    return lax.ppermute(block, axis, [(i, i ^ distance) for i in range(lax.axis_size(axis))])


def after(value, *others):
    return lax.optimization_barrier((value,) + others)[0]


def bits_of(size):
    return [1 << b for b in range(size.bit_length() - 1)]


def reversed_bits(index, size):
    return int(f"{index + size:b}"[:0:-1], 2) if size > 1 else 0


def gather_rows(block, between=None):
    stack = block[None]
    for distance in reversed(bits_of(lax.axis_size("tensor"))):
        arrived = swapped(stack, "tensor", distance)
        if between is not None:
            arrived = after(arrived, *between(arrived))
            between = None
        stack = jnp.concatenate((stack, arrived))
    return stack


def gather_chunks(block):
    size = lax.axis_size("tensor")
    chunks = {0: block}
    for distance in reversed(bits_of(size)):
        for k in sorted(chunks):
            chunks[k ^ distance] = swapped(chunks[k], "tensor", distance)
    return [chunks[reversed_bits(p, size)] for p in range(size)]


def reduce_rows(partial_of, pieces=1, between=None, hold=(), notes=None):
    size = lax.axis_size("tensor")
    if size == 1:
        return partial_of(0, 1)[0]
    low = size // 2
    step = low // pieces
    arrived = {}
    for start in reversed(range(low, size, step)):
        sent = partial_of(start, start + step).astype(half)
        arrived[start - low] = swapped(sent, "tensor", 1).astype(full)
    sums = {}
    quarter = max(low // 2, 1)
    for start in reversed(range(0, low, quarter)):
        if step >= quarter:
            key = start - start % step
            piece = arrived[key][start - key : start - key + quarter]
        else:
            piece = jnp.concatenate([arrived[k] for k in range(start, start + quarter, step)])
        sums[start] = partial_of(start, start + quarter) + piece
    if low == 1:
        return sums[0][0]
    far, near = sums[quarter], sums[0]
    distance = 2
    while True:
        sent = far.astype(half)
        (near,) = lax.optimization_barrier((near,))
        if notes is not None:
            notes["sent"], notes["near"] = sent, near
        if hold:
            sent = after(sent, *hold)
            hold = ()
        arrived = swapped(sent, "tensor", distance)
        if notes is not None:
            notes["arrived"] = arrived
            notes = None
        if between is not None:
            arrived = after(arrived, *between(sent, near))
            between = None
        near = near + arrived.astype(full)
        if near.shape[0] == 1:
            return near[0]
        distance *= 2
        middle = near.shape[0] // 2
        far, near = near[middle:], near[:middle]


def ring_of():
    rows, columns = lax.axis_size("dp"), lax.axis_size("seq")
    ring = []
    for r in range(rows):
        line = [r * columns + c for c in range(columns)]
        ring += line if r % 2 == 0 else line[::-1]
    return ring


def ring_neighbour(ring, offset):
    size = len(ring)
    table = [0] * size
    for place, index in enumerate(ring):
        table[index] = ring[(place + offset) % size]
    return jnp.array(table, jnp.int32)[lax.axis_index(owners)]


def ring_shift(block, ring, direction):
    size = len(ring)
    return lax.ppermute(
        block, owners, [(ring[p], ring[(p + direction) % size]) for p in range(size)]
    )


def ring_hops(block, ring):
    size = len(ring)
    forward = backward = block
    hops = []
    for hop in range(1, size // 2 + 1):
        forward = ring_shift(forward, ring, 1)
        backward = ring_shift(backward, ring, -1) if hop <= (size - 1) // 2 else None
        hops.append((forward, backward))
    return hops


def ring_place(block, hops, ring):
    rows = block.shape[0]
    result = jnp.zeros((rows * len(ring),) + block.shape[1:], block.dtype)
    pieces = [(0, block)]
    for hop, (forward, backward) in enumerate(hops, 1):
        pieces.append((-hop, forward))
        if backward is not None:
            pieces.append((hop, backward))
    for offset, piece in pieces:
        start = ring_neighbour(ring, offset) * rows
        result = lax.dynamic_update_slice_in_dim(result, piece, start, 0)
    return result


def ring_scatter(partial, holds=()):
    ring = ring_of()
    size = len(ring)
    rows = partial.shape[0] // size

    def piece(offset):
        start = ring_neighbour(ring, offset) * rows
        return lax.dynamic_slice_in_dim(partial, start, rows, 0).astype(full)

    total = piece(0)
    running = {1: None, -1: None}
    for step in range(size // 2):
        for direction, reach in ((1, size // 2), (-1, (size - 1) // 2)):
            hop = reach - step
            if hop <= 0:
                continue
            own = piece(direction * hop)
            if running[direction] is not None:
                own = own + running[direction].astype(full)
            sent = own.astype(half)
            if step < len(holds) and holds[step]:
                sent = after(sent, *holds[step])
            running[direction] = ring_shift(sent, ring, direction)
    for arrived in running.values():
        if arrived is not None:
            total = total + arrived.astype(full)
    return total


def sum_everywhere(block):
    sums = [block]
    for axis in ("tensor", "dp", "seq"):
        for distance in bits_of(lax.axis_size(axis)):
            sums.append(sums[-1] + swapped(sums[-1], axis, distance))
    return sums


def norm_forward(row_values, gain_vector):
    inverse = lax.rsqrt(jnp.mean(row_values * row_values, axis=-1, keepdims=True) + norm_eps)
    normed = row_values * inverse
    return (normed, inverse, normed * gain_vector)


def norm_backward(grad_rows, normed, inverse, gain_vector):
    scaled = grad_rows * gain_vector
    return inverse * (scaled - normed * jnp.mean(scaled * normed, axis=-1, keepdims=True))


def adamw(weight, gradient, first_moment, second_moment, step_rate, decay_factor):
    first_new = beta_one * first_moment + (1.0 - beta_one) * gradient
    second_new = beta_two * second_moment + (1.0 - beta_two) * gradient * gradient
    first_hat = first_new / (1.0 - beta_one**STEP)
    second_hat = second_new / (1.0 - beta_two**STEP)
    weight_new = weight - step_rate * (
        first_hat / (jnp.sqrt(second_hat) + adam_eps) + decay_factor * weight
    )
    return (weight_new, first_new, second_new)


def divisor_tile(extent, unit, most):
    best = extent
    for tile in range(unit, min(extent, most) + 1, unit):
        if extent % tile == 0:
            best = tile
    return best


def feed_kernel(chunks, *refs):
    m_refs, (e_ref, w_ref, d_ref) = refs[:chunks], refs[chunks : chunks + 3]
    v_ref, p_ref = refs[-2:]
    unit_tile = d_ref.shape[1]
    for q in range(chunks):
        both = jnp.dot(m_refs[q][...], w_ref[...], preferred_element_type=full)
        grad_act = jnp.dot(e_ref[q, 0], d_ref[...], preferred_element_type=full)
        gate_pre, up_pre = both[:, :unit_tile], both[:, unit_tile:]
        sigmoid_gate = jax.nn.sigmoid(gate_pre)
        silu_gate = gate_pre * sigmoid_gate
        v_ref[q, 0] = (silu_gate * up_pre).astype(half)
        p_ref[q, 0, :, :unit_tile] = (
            grad_act * up_pre * sigmoid_gate * (1.0 + gate_pre * (1.0 - sigmoid_gate))
        ).astype(half)
        p_ref[q, 0, :, unit_tile:] = (grad_act * silu_gate).astype(half)


def feed_core(m_chunks, e_rows, feed_full, unit_tile, side, held):
    chunks = len(m_chunks)
    count, width = m_chunks[0].shape
    units = feed_full.shape[1] // 3
    steps = units // unit_tile
    down, down_base = feed_full, 2 * steps
    if unit_tile % 128:
        down, down_base = feed_full[:, 2 * units :], 0
    chunk_spec = pl.BlockSpec((count, width), lambda j: (0, 0))

    def row_spec(columns):
        return pl.BlockSpec((chunks, 1, count, columns), lambda j: (0, side, 0, j))

    operands = list(m_chunks) + [e_rows, feed_full, down]
    in_specs = [chunk_spec] * chunks + [
        pl.BlockSpec((chunks, 1, count, width), lambda j: (0, side, 0, 0)),
        pl.BlockSpec((width, 2 * unit_tile), lambda j: (0, j)),
        pl.BlockSpec((width, unit_tile), lambda j: (0, down_base + j)),
    ]
    aliases = {}
    if held is not None:
        aliases = {len(operands) + i: i for i in range(2)}
        operands += list(held)
        in_specs += [pl.BlockSpec(memory_space=pl.ANY)] * 2
    work = chunks * count
    return pl.pallas_call(
        functools.partial(feed_kernel, chunks),
        out_shape=tuple(
            jax.ShapeDtypeStruct((chunks, 2, count, c), half) for c in (units, 2 * units)
        ),
        grid=(steps,),
        in_specs=in_specs,
        out_specs=(row_spec(unit_tile), row_spec(2 * unit_tile)),
        input_output_aliases=aliases,
        cost_estimate=pl.CostEstimate(
            flops=6 * work * width * units,
            bytes_accessed=4 * work * width + 6 * width * units + 6 * work * units,
            transcendentals=work * units,
        ),
        compiler_params=pltpu.CompilerParams(vmem_limit_bytes=56 << 20),
        name="feed_core",
    )(*operands)


def interleave(gate, up, tile):
    pieces = []
    for start in range(0, gate.shape[1], tile):
        pieces += [gate[:, start : start + tile], up[:, start : start + tile]]
    return pieces


def separate(both, tile):
    pieces = [both[:, start : start + tile] for start in range(0, both.shape[1], tile)]
    return jnp.concatenate(pieces[::2], axis=1), jnp.concatenate(pieces[1::2], axis=1)


def on_device(*arguments):
    hidden, out_cotangent = arguments[:2]
    weights, firsts, seconds = (arguments[2 + 8 * i : 10 + 8 * i] for i in range(3))
    (
        mixer_gain,
        input_weight,
        conv_weight,
        output_weight,
        feed_gain,
        gate_weight,
        up_weight,
        down_weight,
    ) = weights
    parts = lax.axis_size("tensor")
    place = lax.axis_index("tensor")
    seqs, rows, width = hidden.shape
    channels = input_weight.shape[2]
    units = gate_weight.shape[1]

    mixer_own = jnp.concatenate(
        [input_weight[:, k].astype(half) for k in range(3)] + [output_weight.T.astype(half)],
        axis=1,
    )
    unit_tile = divisor_tile(units, 128, 384)
    feed_own = jnp.concatenate(
        interleave(gate_weight.astype(half), up_weight.astype(half), unit_tile)
        + [down_weight.T.astype(half)],
        axis=1,
    )
    feed_full = lax.all_gather(feed_own, owners, axis=0, tiled=True)
    ring = ring_of()
    hops = ring_hops(mixer_own, ring)
    mixer_full = ring_place(mixer_own, hops, ring)
    input_full = mixer_full[:, : 3 * channels]
    output_full = mixer_full[:, 3 * channels :]

    channel_start = place * channels
    taps = lax.dynamic_slice_in_dim(conv_weight, channel_start, channels, 1)
    normed_one, inverse_one, scaled_one = norm_forward(hidden, mixer_gain)
    first_half, last_hop = (hops[min(1, len(hops) - 1)], hops[-1]) if hops else ((None,), (None,))
    gathered = {}

    def ring_first(arrived):
        gathered["a"] = arrived
        return tuple(h for h in first_half if h is not None)

    def mixer_first(arrived):
        gathered["e"] = arrived
        return tuple(h for h in last_hop if h is not None)

    mixer_rows = gather_rows(scaled_one.astype(half), ring_first)
    out_rows = gather_rows(
        after(out_cotangent.astype(half), *([gathered["a"]] if gathered else [])), mixer_first
    )
    projected = jnp.einsum("kstd,de->kste", mixer_rows, input_full, preferred_element_type=full)
    part_b = projected[..., :channels]
    part_c = projected[..., channels : 2 * channels]
    part_x = projected[..., 2 * channels :]
    gated_in = (part_b * part_x).astype(half)

    places = [place ^ reversed_bits(p, parts) for p in range(parts)]

    def pick(pieces, wanted):
        chosen = jnp.zeros_like(pieces[0])
        for k in range(parts):
            chosen = jnp.where(places[k] == wanted, pieces[k], chosen)
        return chosen

    tails = [gated_in[k, :, rows - 2 :] for k in range(parts)]
    carried = shifted(pick(tails, parts - 1), "seq", 1)
    before = jnp.stack(
        [
            jnp.where(places[k] == 0, carried, pick(tails, places[k] - 1))
            for k in range(parts)
        ]
    )
    padded = jnp.concatenate((before, gated_in), axis=2).astype(full)
    conv_out = (
        taps[0] * padded[:, :, :rows]
        + taps[1] * padded[:, :, 1 : rows + 1]
        + taps[2] * padded[:, :, 2:]
    )
    mixed_out = (part_c * conv_out).astype(half)
    if "e" in gathered:
        mixed_out = after(mixed_out, gathered["e"])

    def narrow(pattern, left, right):
        return jnp.einsum(pattern, left, right, preferred_element_type=full)

    branch = reduce_rows(
        lambda low, high: narrow("kstc,dc->kstd", mixed_out[low:high], output_full)
    )
    middle = hidden + branch

    normed_two, inverse_two, scaled_two = norm_forward(middle, feed_gain)
    chunk_rows = seqs * rows
    feed_sent = after(scaled_two.astype(half), out_rows)
    feed_chunks = gather_chunks(feed_sent.reshape(chunk_rows, width))
    e_rows = out_rows.reshape(parts // 2, 2, chunk_rows, width)
    held = None
    for side in range(2):
        held = feed_core(feed_chunks[side::2], e_rows, feed_full, unit_tile, side, held)
    activated, grad_pre = (h.reshape((parts, chunk_rows, h.shape[-1])) for h in held)
    gate_up_full = feed_full[:, : 2 * units]
    down_full = feed_full[:, 2 * units :]
    feed_rows = jnp.stack(feed_chunks)

    def feed_back(low, high):
        return narrow("ktf,df->ktd", grad_pre[low:high], gate_up_full)

    e_flat = out_rows.reshape(parts, chunk_rows, width)
    grads = {}

    def weight_grads(sent, near):
        left, right = after(feed_rows, sent, near), after(e_flat, sent, near)
        grads["gate_up"] = narrow("ktd,ktf->df", left, grad_pre).astype(half)
        grads["down"] = narrow("ktd,ktf->df", right, activated).astype(half)
        return (grads["gate_up"], grads["down"])

    grad_scaled_two = reduce_rows(feed_back, 2, weight_grads).reshape(seqs, rows, width)
    if not grads:
        weight_grads(grad_scaled_two, grad_scaled_two)
    feed_gain_part = jnp.sum(grad_scaled_two * normed_two, axis=(0, 1))
    grad_middle = out_cotangent + norm_backward(
        grad_scaled_two, normed_two, inverse_two, feed_gain
    )
    middle_sent = grad_middle.astype(half)
    grad_feed = jnp.concatenate((grads["gate_up"], grads["down"]), axis=1)
    owned_feed = lax.psum_scatter(
        grad_feed, owners, scatter_dimension=0, tiled=True
    ).astype(full)
    owned_gate_up, owned_down = owned_feed[:, : 2 * units], owned_feed[:, 2 * units :].T
    sums = {}

    def feed_output(arrived):
        held_back = after(activated, grad_feed, middle_sent)
        sums["f"] = reduce_rows(
            lambda low, high: narrow("ktf,df->ktd", held_back[low:high], down_full),
            hold=(arrived,),
            notes=sums,
        )
        return tuple(sums[key] for key in ("sent", "near") if key in sums)

    middle_rows = gather_rows(middle_sent, feed_output)
    if not sums:
        feed_output(middle_sent)
    block_output = middle + sums["f"].reshape(seqs, rows, width)

    grad_mixed = narrow("kstd,dc->kstc", middle_rows, output_full)
    grad_output = narrow("kstd,kstc->dc", middle_rows, mixed_out).astype(half)
    grad_c = grad_mixed * conv_out
    grad_conv_out = grad_mixed * part_c
    conv_part = jnp.stack(
        [
            jnp.sum(grad_conv_out * padded[:, :, tap : tap + rows], axis=(0, 1, 2))
            for tap in range(3)
        ]
    )
    heads = [grad_conv_out[k, :, :2] for k in range(parts)]
    following = after(shifted(pick(heads, 0), "seq", -1), grad_output)
    following_rows = jnp.stack(
        [
            jnp.where(places[k] == parts - 1, following, pick(heads, places[k] + 1))
            for k in range(parts)
        ]
    )
    conv_tail = jnp.concatenate((grad_conv_out, following_rows), axis=2)
    grad_gated = (
        taps[0] * conv_tail[:, :, 2:]
        + taps[1] * conv_tail[:, :, 1 : rows + 1]
        + taps[2] * conv_tail[:, :, :rows]
    )
    grad_projected = jnp.concatenate(
        (
            (grad_gated * part_x).astype(half),
            grad_c.astype(half),
            (grad_gated * part_b).astype(half),
        ),
        axis=-1,
    )
    if "arrived" in sums:
        grad_projected = after(grad_projected, sums["arrived"])
    grad_input = narrow("kstd,kste->de", mixer_rows, grad_projected).astype(half)
    grad_mixer = jnp.concatenate((grad_input, grad_output), axis=1)
    (grad_mixer,) = lax.optimization_barrier((grad_mixer,))
    mixer_gain_part = (
        jnp.sum(
            grad_mixer[:, : 3 * channels].astype(full) * input_full.astype(full), axis=1
        )
        / mixer_gain
    )
    conv_placed = lax.dynamic_update_slice_in_dim(
        jnp.zeros(conv_weight.shape, full), conv_part, channel_start, 1
    )
    vector_sums = sum_everywhere(
        jnp.concatenate((mixer_gain_part[None], feed_gain_part[None], conv_placed), axis=0)
    )
    vectors = vector_sums[-1]
    steps = {}

    def back_product(low, high):
        steps[low] = narrow("kste,de->kstd", grad_projected[low:high], input_full)
        return steps[low]

    grad_scaled_one = reduce_rows(back_product, notes=steps)
    odd = [steps[parts // 2].astype(half)] if parts // 2 in steps else []
    far = [steps["sent"], steps["near"]] if "sent" in steps else []
    owned_mixer = ring_scatter(
        grad_mixer,
        ((), odd + vector_sums[1:2], far + vector_sums[2:3], vector_sums[3:4]),
    )
    hidden_grad = grad_middle + norm_backward(
        grad_scaled_one, normed_one, inverse_one, mixer_gain
    )

    owned_gate, owned_up = separate(owned_gate_up, unit_tile)
    gradients = (
        vectors[0],
        jnp.stack(
            [owned_mixer[:, k * channels : (k + 1) * channels] for k in range(3)], axis=1
        ),
        vectors[2:],
        owned_mixer[:, 3 * channels :].T,
        vectors[1],
        owned_gate,
        owned_up,
        owned_down,
    )
    vector_flags = (True, False, True, False, True, False, False, False)
    updated = [
        adamw(
            weight,
            gradient,
            first,
            second,
            vector_rate if flag else matrix_rate,
            0.0 if flag else decay_rate,
        )
        for weight, gradient, first, second, flag in zip(
            weights, gradients, firsts, seconds, vector_flags
        )
    ]
    return (
        (block_output, hidden_grad)
        + gradients
        + tuple(u[0] for u in updated)
        + tuple(u[1] for u in updated)
        + tuple(u[2] for u in updated)
    )


def solution(mesh):
    row_spec = P("dp", ("seq", "tensor"), None)
    weight_specs = (
        P(),
        P(owners, None, "tensor"),
        P(),
        P("tensor", owners),
        P(),
        P(owners, "tensor"),
        P(owners, "tensor"),
        P("tensor", owners),
    )
    in_specs = (row_spec, row_spec) + weight_specs * 3
    out_specs = (row_spec, row_spec) + weight_specs * 4
    return jax.shard_map(
        on_device, mesh=mesh, in_specs=in_specs, out_specs=out_specs, check_vma=False
    )
```

```python
import functools

import jax
import jax.numpy as jnp
from jax import lax
from jax.experimental import pallas as pl
from jax.experimental.layout import Layout, with_layout_constraint
from jax.experimental.pallas import tpu as pltpu
from jax.sharding import PartitionSpec as P


STEP = 3

norm_eps = 1e-05
beta_one = 0.9
beta_two = 0.95
adam_eps = 1e-08
matrix_rate = 0.005
vector_rate = 0.05
decay_rate = 0.1

half = jnp.bfloat16
full = jnp.float32
owners = ("dp", "seq")


def shifted(block, axis, distance):
    devices = range(lax.axis_size(axis))
    route = [(i - distance, i) for i in devices if i - distance in devices]
    return lax.ppermute(block, axis, route)


def swapped(block, axis, distance):
    return lax.ppermute(block, axis, [(i, i ^ distance) for i in range(lax.axis_size(axis))])


def after(value, *others):
    return lax.optimization_barrier((value,) + others)[0]


def bits_of(size):
    return [1 << b for b in range(size.bit_length() - 1)]


def reversed_bits(index, size):
    return int(f"{index + size:b}"[:0:-1], 2) if size > 1 else 0


def gather_rows(block, between=None, joined=True):
    stack, arrived = block[None], None
    for distance in reversed(bits_of(lax.axis_size("tensor"))):
        if arrived is not None:
            stack = jnp.concatenate((stack, arrived))
        arrived = swapped(stack, "tensor", distance)
        if between is not None:
            arrived = after(arrived, *between(arrived))
            between = None
    if not joined:
        return stack, arrived
    return stack if arrived is None else jnp.concatenate((stack, arrived))


def gather_chunks(block):
    size = lax.axis_size("tensor")
    chunks = {0: block}
    for distance in reversed(bits_of(size)):
        for k in sorted(chunks):
            chunks[k ^ distance] = swapped(chunks[k], "tensor", distance)
    return [chunks[reversed_bits(p, size)] for p in range(size)]


def reduce_rows(partial_of, pieces=1, between=None, hold=(), notes=None):
    size = lax.axis_size("tensor")
    if size == 1:
        return partial_of(0, 1)[0]
    low = size // 2
    step = low // pieces
    arrived = {}
    for start in reversed(range(low, size, step)):
        sent = partial_of(start, start + step).astype(half)
        arrived[start - low] = swapped(sent, "tensor", 1).astype(full)
    sums = {}
    quarter = max(low // 2, 1)
    for start in reversed(range(0, low, quarter)):
        if step >= quarter:
            key = start - start % step
            piece = arrived[key][start - key : start - key + quarter]
        else:
            piece = jnp.concatenate([arrived[k] for k in range(start, start + quarter, step)])
        sums[start] = partial_of(start, start + quarter) + piece
    if low == 1:
        return sums[0][0]
    far, near = sums[quarter], sums[0]
    distance = 2
    while True:
        sent = far.astype(half)
        (near,) = lax.optimization_barrier((near,))
        if notes is not None:
            notes["sent"], notes["near"] = sent, near
        if hold:
            sent = after(sent, *hold)
            hold = ()
        arrived = swapped(sent, "tensor", distance)
        if notes is not None:
            notes["arrived"] = arrived
            notes = None
        if between is not None:
            arrived = after(arrived, *between(sent, near))
            between = None
        near = near + arrived.astype(full)
        if near.shape[0] == 1:
            return near[0]
        distance *= 2
        middle = near.shape[0] // 2
        far, near = near[middle:], near[:middle]


def ring_of():
    rows, columns = lax.axis_size("dp"), lax.axis_size("seq")
    ring = []
    for r in range(rows):
        line = [r * columns + c for c in range(columns)]
        ring += line if r % 2 == 0 else line[::-1]
    return ring


def ring_neighbour(ring, offset):
    size = len(ring)
    table = [0] * size
    for place, index in enumerate(ring):
        table[index] = ring[(place + offset) % size]
    return jnp.array(table, jnp.int32)[lax.axis_index(owners)]


def ring_shift(block, ring, direction):
    size = len(ring)
    return lax.ppermute(
        block, owners, [(ring[p], ring[(p + direction) % size]) for p in range(size)]
    )


def ring_hops(block, ring):
    size = len(ring)
    forward = backward = block
    hops = []
    for hop in range(1, size // 2 + 1):
        forward = ring_shift(forward, ring, 1)
        backward = ring_shift(backward, ring, -1) if hop <= (size - 1) // 2 else None
        hops.append((forward, backward))
    return hops


def ring_place(block, hops, ring):
    rows = block.shape[0]
    result = jnp.zeros((rows * len(ring),) + block.shape[1:], block.dtype)
    pieces = [(0, block)]
    for hop, (forward, backward) in enumerate(hops, 1):
        pieces.append((-hop, forward))
        if backward is not None:
            pieces.append((hop, backward))
    for offset, piece in pieces:
        start = ring_neighbour(ring, offset) * rows
        result = lax.dynamic_update_slice_in_dim(result, piece, start, 0)
    return result


def ring_scatter(partials, holds=()):
    ring = ring_of()
    size = len(ring)
    rows = partials[0].shape[0] // size

    def piece(offset):
        start = ring_neighbour(ring, offset) * rows
        return jnp.concatenate(
            [lax.dynamic_slice_in_dim(p, start, rows, 0) for p in partials], axis=1
        ).astype(full)

    total = piece(0)
    running = {1: None, -1: None}
    for step in range(size // 2):
        for direction, reach in ((1, size // 2), (-1, (size - 1) // 2)):
            hop = reach - step
            if hop <= 0:
                continue
            own = piece(direction * hop)
            if running[direction] is not None:
                own = own + running[direction].astype(full)
            sent = own.astype(half)
            if step < len(holds) and holds[step]:
                sent = after(sent, *holds[step])
            running[direction] = ring_shift(sent, ring, direction)
    for arrived in running.values():
        if arrived is not None:
            total = total + arrived.astype(full)
    return total


def sum_everywhere(block):
    sums = [block]
    for axis in ("tensor", "dp", "seq"):
        for distance in bits_of(lax.axis_size(axis)):
            sums.append(sums[-1] + swapped(sums[-1], axis, distance))
    return sums


def norm_forward(row_values, gain_vector):
    inverse = lax.rsqrt(jnp.mean(row_values * row_values, axis=-1, keepdims=True) + norm_eps)
    normed = row_values * inverse
    return (normed, inverse, normed * gain_vector)


def norm_backward(grad_rows, normed, inverse, gain_vector):
    scaled = grad_rows * gain_vector
    return inverse * (scaled - normed * jnp.mean(scaled * normed, axis=-1, keepdims=True))


def adamw(weight, gradient, first_moment, second_moment, step_rate, decay_factor):
    first_new = beta_one * first_moment + (1.0 - beta_one) * gradient
    second_new = beta_two * second_moment + (1.0 - beta_two) * gradient * gradient
    first_hat = first_new / (1.0 - beta_one**STEP)
    second_hat = second_new / (1.0 - beta_two**STEP)
    weight_new = weight - step_rate * (
        first_hat / (jnp.sqrt(second_hat) + adam_eps) + decay_factor * weight
    )
    return (weight_new, first_new, second_new)


def upright(matrix):
    return with_layout_constraint(matrix, Layout(major_to_minor=(0, 1)))


def divisor_tile(extent, unit, most):
    best = extent
    for tile in range(unit, min(extent, most) + 1, unit):
        if extent % tile == 0:
            best = tile
    return best


def feed_kernel(chunks, *refs):
    m_refs, e_refs = refs[:chunks], refs[chunks : 2 * chunks]
    w_ref, d_ref = refs[2 * chunks : 2 * chunks + 2]
    v_ref, p_ref = refs[-2:]
    unit_tile = d_ref.shape[1]
    for q in range(chunks):
        both = jnp.dot(m_refs[q][...], w_ref[...], preferred_element_type=full)
        grad_act = jnp.dot(e_refs[q][0], d_ref[...], preferred_element_type=full)
        gate_pre, up_pre = both[:, :unit_tile], both[:, unit_tile:]
        sigmoid_gate = jax.nn.sigmoid(gate_pre)
        silu_gate = gate_pre * sigmoid_gate
        v_ref[q, 0] = (silu_gate * up_pre).astype(half)
        p_ref[q, 0, :, :unit_tile] = (
            grad_act * up_pre * sigmoid_gate * (1.0 + gate_pre * (1.0 - sigmoid_gate))
        ).astype(half)
        p_ref[q, 0, :, unit_tile:] = (grad_act * silu_gate).astype(half)


def feed_core(m_chunks, e_parts, feed_full, unit_tile, side, held):
    chunks = len(m_chunks)
    count, width = m_chunks[0].shape
    units = feed_full.shape[1] // 3
    steps = units // unit_tile
    down, down_base = feed_full, 2 * steps
    if unit_tile % 128:
        down, down_base = feed_full[:, 2 * units :], 0
    chunk_spec = pl.BlockSpec((count, width), lambda j: (0, 0))

    def row_spec(columns):
        return pl.BlockSpec((chunks, 1, count, columns), lambda j: (0, side, 0, j))

    held_rows = e_parts[0].shape[0]
    e_places = [divmod(2 * q + side, held_rows) for q in range(chunks)]
    operands = list(m_chunks) + [e_parts[part] for part, _ in e_places] + [feed_full, down]
    in_specs = [chunk_spec] * chunks
    in_specs += [
        pl.BlockSpec((1, count, width), lambda j, row=row: (row, 0, 0)) for _, row in e_places
    ]
    in_specs += [
        pl.BlockSpec((width, 2 * unit_tile), lambda j: (0, j)),
        pl.BlockSpec((width, unit_tile), lambda j: (0, down_base + j)),
    ]
    aliases = {}
    if held is not None:
        aliases = {len(operands) + i: i for i in range(2)}
        operands += list(held)
        in_specs += [pl.BlockSpec(memory_space=pl.ANY)] * 2
    work = chunks * count
    return pl.pallas_call(
        functools.partial(feed_kernel, chunks),
        out_shape=tuple(
            jax.ShapeDtypeStruct((chunks, 2, count, c), half) for c in (units, 2 * units)
        ),
        grid=(steps,),
        in_specs=in_specs,
        out_specs=(row_spec(unit_tile), row_spec(2 * unit_tile)),
        input_output_aliases=aliases,
        cost_estimate=pl.CostEstimate(
            flops=6 * work * width * units,
            bytes_accessed=4 * work * width + 6 * width * units + 6 * work * units,
            transcendentals=work * units,
        ),
        compiler_params=pltpu.CompilerParams(vmem_limit_bytes=56 << 20),
        name="feed_core",
    )(*operands)


def interleave(gate, up, tile):
    pieces = []
    for start in range(0, gate.shape[1], tile):
        pieces += [gate[:, start : start + tile], up[:, start : start + tile]]
    return pieces


def separate(both, tile):
    pieces = [both[:, start : start + tile] for start in range(0, both.shape[1], tile)]
    return jnp.concatenate(pieces[::2], axis=1), jnp.concatenate(pieces[1::2], axis=1)


def on_device(*arguments):
    hidden, out_cotangent = arguments[:2]
    weights, firsts, seconds = (arguments[2 + 8 * i : 10 + 8 * i] for i in range(3))
    (
        mixer_gain,
        input_weight,
        conv_weight,
        output_weight,
        feed_gain,
        gate_weight,
        up_weight,
        down_weight,
    ) = weights
    parts = lax.axis_size("tensor")
    place = lax.axis_index("tensor")
    seqs, rows, width = hidden.shape
    channels = input_weight.shape[2]
    units = gate_weight.shape[1]

    mixer_own = jnp.concatenate(
        [input_weight[:, k].astype(half) for k in range(3)] + [output_weight.T.astype(half)],
        axis=1,
    )
    unit_tile = divisor_tile(units, 128, 384)
    feed_own = jnp.concatenate(
        interleave(gate_weight.astype(half), up_weight.astype(half), unit_tile)
        + [down_weight.T.astype(half)],
        axis=1,
    )
    ring = ring_of()
    hops = ring_hops(mixer_own, ring)
    mixer_full = ring_place(mixer_own, hops, ring)
    input_full = mixer_full[:, : 3 * channels]
    output_full = mixer_full[:, 3 * channels :]

    feed_full = ring_place(feed_own, ring_hops(feed_own, ring), ring)

    channel_start = place * channels
    taps = lax.dynamic_slice_in_dim(conv_weight, channel_start, channels, 1)
    normed_one, inverse_one, scaled_one = norm_forward(hidden, mixer_gain)
    first_half, last_hop = (hops[min(1, len(hops) - 1)], hops[-1]) if hops else ((None,), (None,))
    gathered = {}

    def ring_first(arrived):
        gathered["a"] = arrived
        return tuple(h for h in first_half if h is not None)

    def mixer_first(arrived):
        gathered["e"] = arrived
        return tuple(h for h in last_hop if h is not None)

    mixer_rows = gather_rows(scaled_one.astype(half), ring_first)
    out_parts = [
        part.reshape(part.shape[0], seqs * rows, width)
        for part in gather_rows(
            after(out_cotangent.astype(half), *([gathered["a"]] if gathered else [])),
            mixer_first,
            joined=False,
        )
        if part is not None
    ]
    projected = jnp.einsum("kstd,de->kste", mixer_rows, input_full, preferred_element_type=full)
    part_b = projected[..., :channels]
    part_c = projected[..., channels : 2 * channels]
    part_x = projected[..., 2 * channels :]
    gated_in = (part_b * part_x).astype(half)

    places = [place ^ reversed_bits(p, parts) for p in range(parts)]

    def pick(pieces, wanted):
        chosen = jnp.zeros_like(pieces[0])
        for k in range(parts):
            chosen = jnp.where(places[k] == wanted, pieces[k], chosen)
        return chosen

    tails = [gated_in[k, :, rows - 2 :] for k in range(parts)]
    carried = shifted(pick(tails, parts - 1), "seq", 1)
    before = jnp.stack(
        [
            jnp.where(places[k] == 0, carried, pick(tails, places[k] - 1))
            for k in range(parts)
        ]
    )
    padded = jnp.concatenate((before, gated_in), axis=2).astype(full)
    conv_out = (
        taps[0] * padded[:, :, :rows]
        + taps[1] * padded[:, :, 1 : rows + 1]
        + taps[2] * padded[:, :, 2:]
    )
    mixed_out = (part_c * conv_out).astype(half)
    if "e" in gathered:
        mixed_out = after(mixed_out, gathered["e"])

    def narrow(pattern, left, right):
        return jnp.einsum(pattern, left, right, preferred_element_type=full)

    branch = reduce_rows(
        lambda low, high: narrow("kstc,dc->kstd", mixed_out[low:high], output_full)
    )
    middle = hidden + branch

    normed_two, inverse_two, scaled_two = norm_forward(middle, feed_gain)
    chunk_rows = seqs * rows
    feed_sent = after(scaled_two.astype(half), *out_parts)
    feed_chunks = gather_chunks(feed_sent.reshape(chunk_rows, width))
    held = None
    for side in range(2):
        held = feed_core(feed_chunks[side::2], out_parts, feed_full, unit_tile, side, held)
    activated, grad_pre = (h.reshape((parts, chunk_rows, h.shape[-1])) for h in held)
    gate_up_full = feed_full[:, : 2 * units]
    down_full = feed_full[:, 2 * units :]

    def feed_back(low, high):
        return narrow("ktf,df->ktd", grad_pre[low:high], gate_up_full)

    grads = {}

    def weight_grads(sent, near):
        left = jnp.stack([after(c, sent, near) for c in feed_chunks])
        right = jnp.concatenate([after(p, sent, near) for p in out_parts])
        grads["gate_up"] = upright(narrow("ktd,ktf->df", left, grad_pre).astype(half))
        grads["down"] = upright(narrow("ktd,ktf->df", right, activated).astype(half))
        return (grads["gate_up"], grads["down"])

    grad_scaled_two = reduce_rows(feed_back, 2, weight_grads).reshape(seqs, rows, width)
    if not grads:
        weight_grads(grad_scaled_two, grad_scaled_two)
    feed_gain_part = jnp.sum(grad_scaled_two * normed_two, axis=(0, 1))
    grad_middle = out_cotangent + norm_backward(
        grad_scaled_two, normed_two, inverse_two, feed_gain
    )
    middle_sent = grad_middle.astype(half)
    owned_feed = upright(ring_scatter((grads["gate_up"], grads["down"])))
    owned_gate_up, owned_down = owned_feed[:, : 2 * units], upright(owned_feed[:, 2 * units :].T)
    sums = {}

    def feed_output(arrived):
        held_back = after(activated, grads["gate_up"], grads["down"], middle_sent)
        sums["f"] = reduce_rows(
            lambda low, high: narrow("ktf,df->ktd", held_back[low:high], down_full),
            hold=(arrived,),
            notes=sums,
        )
        return tuple(sums[key] for key in ("sent", "near") if key in sums)

    middle_rows = gather_rows(middle_sent, feed_output)
    if not sums:
        feed_output(middle_sent)
    block_output = middle + sums["f"].reshape(seqs, rows, width)

    grad_mixed = narrow("kstd,dc->kstc", middle_rows, output_full)
    grad_output = narrow("kstd,kstc->dc", middle_rows, mixed_out).astype(half)
    grad_c = grad_mixed * conv_out
    grad_conv_out = grad_mixed * part_c
    conv_part = jnp.stack(
        [
            jnp.sum(grad_conv_out * padded[:, :, tap : tap + rows], axis=(0, 1, 2))
            for tap in range(3)
        ]
    )
    heads = [grad_conv_out[k, :, :2] for k in range(parts)]
    following = after(shifted(pick(heads, 0), "seq", -1), grad_output)
    following_rows = jnp.stack(
        [
            jnp.where(places[k] == parts - 1, following, pick(heads, places[k] + 1))
            for k in range(parts)
        ]
    )
    conv_tail = jnp.concatenate((grad_conv_out, following_rows), axis=2)
    grad_gated = (
        taps[0] * conv_tail[:, :, 2:]
        + taps[1] * conv_tail[:, :, 1 : rows + 1]
        + taps[2] * conv_tail[:, :, :rows]
    )
    grad_projected = jnp.concatenate(
        (
            (grad_gated * part_x).astype(half),
            grad_c.astype(half),
            (grad_gated * part_b).astype(half),
        ),
        axis=-1,
    )
    if "arrived" in sums:
        grad_projected = after(grad_projected, sums["arrived"])
    grad_input = narrow("kstd,kste->de", mixer_rows, grad_projected).astype(half)
    (grad_input,) = lax.optimization_barrier((upright(grad_input),))
    mixer_gain_part = (
        jnp.sum(grad_input.astype(full) * input_full.astype(full), axis=1)
        / mixer_gain
    )
    conv_placed = lax.dynamic_update_slice_in_dim(
        jnp.zeros(conv_weight.shape, full), conv_part, channel_start, 1
    )
    vector_sums = sum_everywhere(
        jnp.concatenate((mixer_gain_part[None], feed_gain_part[None], conv_placed), axis=0)
    )
    vectors = vector_sums[-1]
    steps = {}

    def back_product(low, high):
        steps[low] = narrow("kste,de->kstd", grad_projected[low:high], input_full)
        return steps[low]

    grad_scaled_one = reduce_rows(back_product, notes=steps)
    far = [steps["sent"], steps["near"]] if "sent" in steps else []
    owned_mixer = upright(ring_scatter((grad_input, upright(grad_output)), ((), far)))
    hidden_grad = grad_middle + norm_backward(
        grad_scaled_one, normed_one, inverse_one, mixer_gain
    )

    owned_gate, owned_up = separate(owned_gate_up, unit_tile)
    gradients = (
        vectors[0],
        jnp.stack(
            [owned_mixer[:, k * channels : (k + 1) * channels] for k in range(3)], axis=1
        ),
        vectors[2:],
        upright(owned_mixer[:, 3 * channels :].T),
        vectors[1],
        owned_gate,
        owned_up,
        owned_down,
    )
    vector_flags = (True, False, True, False, True, False, False, False)
    updated = [
        adamw(
            weight,
            gradient,
            first,
            second,
            vector_rate if flag else matrix_rate,
            0.0 if flag else decay_rate,
        )
        for weight, gradient, first, second, flag in zip(
            weights, gradients, firsts, seconds, vector_flags
        )
    ]
    return (
        (block_output, hidden_grad)
        + gradients
        + tuple(u[0] for u in updated)
        + tuple(u[1] for u in updated)
        + tuple(u[2] for u in updated)
    )


def solution(mesh):
    row_spec = P("dp", ("seq", "tensor"), None)
    weight_specs = (
        P(),
        P(owners, None, "tensor"),
        P(),
        P("tensor", owners),
        P(),
        P(owners, "tensor"),
        P(owners, "tensor"),
        P("tensor", owners),
    )
    in_specs = (row_spec, row_spec) + weight_specs * 3
    out_specs = (row_spec, row_spec) + weight_specs * 4
    return jax.shard_map(
        on_device, mesh=mesh, in_specs=in_specs, out_specs=out_specs, check_vma=False
    )
```

```python
import functools

import jax
import jax.numpy as jnp
from jax import lax
from jax.experimental import pallas as pl
from jax.experimental.layout import Layout, with_layout_constraint
from jax.experimental.pallas import tpu as pltpu
from jax.sharding import PartitionSpec as P


STEP = 3

norm_eps = 1e-05
beta_one = 0.9
beta_two = 0.95
adam_eps = 1e-08
matrix_rate = 0.005
vector_rate = 0.05
decay_rate = 0.1

half = jnp.bfloat16
full = jnp.float32
owners = ("dp", "seq")


def shifted(block, axis, distance):
    devices = range(lax.axis_size(axis))
    route = [(i - distance, i) for i in devices if i - distance in devices]
    return lax.ppermute(block, axis, route)


def swapped(block, axis, distance):
    return lax.ppermute(block, axis, [(i, i ^ distance) for i in range(lax.axis_size(axis))])


def after(value, *others):
    return lax.optimization_barrier((value,) + others)[0]


def bits_of(size):
    return [1 << b for b in range(size.bit_length() - 1)]


def reversed_bits(index, size):
    return int(f"{index + size:b}"[:0:-1], 2) if size > 1 else 0


def gather_rows(block, between=None, joined=True):
    stack, arrived = block[None], None
    for distance in reversed(bits_of(lax.axis_size("tensor"))):
        if arrived is not None:
            stack = jnp.concatenate((stack, arrived))
        arrived = swapped(stack, "tensor", distance)
        if between is not None:
            arrived = after(arrived, *between(arrived))
            between = None
    if not joined:
        return stack, arrived
    return stack if arrived is None else jnp.concatenate((stack, arrived))


def gather_chunks(block):
    size = lax.axis_size("tensor")
    chunks = {0: block}
    for distance in reversed(bits_of(size)):
        for k in sorted(chunks):
            chunks[k ^ distance] = swapped(chunks[k], "tensor", distance)
    return [chunks[reversed_bits(p, size)] for p in range(size)]


def reduce_rows(partial_of, pieces=1, between=None, hold=(), notes=None):
    size = lax.axis_size("tensor")
    if size == 1:
        return partial_of(0, 1)[0]
    low = size // 2
    step = low // pieces
    arrived = {}
    for start in reversed(range(low, size, step)):
        sent = partial_of(start, start + step).astype(half)
        arrived[start - low] = swapped(sent, "tensor", 1).astype(full)
    sums = {}
    quarter = max(low // 2, 1)
    for start in reversed(range(0, low, quarter)):
        if step >= quarter:
            key = start - start % step
            piece = arrived[key][start - key : start - key + quarter]
        else:
            piece = jnp.concatenate([arrived[k] for k in range(start, start + quarter, step)])
        sums[start] = partial_of(start, start + quarter) + piece
    if low == 1:
        return sums[0][0]
    far, near = sums[quarter], sums[0]
    distance = 2
    while True:
        sent = far.astype(half)
        (near,) = lax.optimization_barrier((near,))
        if notes is not None:
            notes["sent"], notes["near"] = sent, near
        if hold:
            sent = after(sent, *hold)
            hold = ()
        arrived = swapped(sent, "tensor", distance)
        if notes is not None:
            notes["arrived"] = arrived
            notes = None
        if between is not None:
            arrived = after(arrived, *between(sent, near))
            between = None
        near = near + arrived.astype(full)
        if near.shape[0] == 1:
            return near[0]
        distance *= 2
        middle = near.shape[0] // 2
        far, near = near[middle:], near[:middle]


def ring_of():
    rows, columns = lax.axis_size("dp"), lax.axis_size("seq")
    ring = []
    for r in range(rows):
        line = [r * columns + c for c in range(columns)]
        ring += line if r % 2 == 0 else line[::-1]
    return ring


def ring_neighbour(ring, offset):
    size = len(ring)
    table = [0] * size
    for place, index in enumerate(ring):
        table[index] = ring[(place + offset) % size]
    return jnp.array(table, jnp.int32)[lax.axis_index(owners)]


def ring_shift(block, ring, direction):
    size = len(ring)
    return lax.ppermute(
        block, owners, [(ring[p], ring[(p + direction) % size]) for p in range(size)]
    )


def ring_hops(block, ring):
    size = len(ring)
    forward = backward = block
    hops = []
    for hop in range(1, size // 2 + 1):
        forward = ring_shift(forward, ring, 1)
        backward = ring_shift(backward, ring, -1) if hop <= (size - 1) // 2 else None
        hops.append((forward, backward))
    return hops


def ring_place(block, hops, ring):
    rows = block.shape[0]
    result = jnp.zeros((rows * len(ring),) + block.shape[1:], block.dtype)
    pieces = [(0, block)]
    for hop, (forward, backward) in enumerate(hops, 1):
        pieces.append((-hop, forward))
        if backward is not None:
            pieces.append((hop, backward))
    for offset, piece in pieces:
        start = ring_neighbour(ring, offset) * rows
        result = lax.dynamic_update_slice_in_dim(result, piece, start, 0)
    return result


def ring_scatter(partials, holds=(), reads=()):
    ring = ring_of()
    size = len(ring)
    rows = partials[0].shape[0] // size

    def piece(offset):
        start = ring_neighbour(ring, offset) * rows
        return jnp.concatenate(
            [lax.dynamic_slice_in_dim(p, start, rows, 0) for p in partials], axis=1
        ).astype(full)

    total = piece(0)
    running = {1: None, -1: None}
    for step in range(size // 2):
        for direction, reach in ((1, size // 2), (-1, (size - 1) // 2)):
            hop = reach - step
            if hop <= 0:
                continue
            own = piece(direction * hop)
            if running[direction] is not None:
                addend = running[direction]
                if step < len(reads) and reads[step]:
                    addend = after(addend, *reads[step])
                own = own + addend.astype(full)
            sent = own.astype(half)
            if step < len(holds) and holds[step]:
                sent = after(sent, *holds[step])
            running[direction] = ring_shift(sent, ring, direction)
    for arrived in running.values():
        if arrived is not None:
            total = total + arrived.astype(full)
    return total


def sum_everywhere(block):
    hops = [(axis, d) for axis in ("tensor", "dp", "seq") for d in bits_of(lax.axis_size(axis))]
    hops.sort(key=lambda hop: hop[0] == "tensor" and hop[1] > 1)
    for axis, distance in hops:
        block = block + swapped(block, axis, distance)
    return block


def norm_forward(row_values, gain_vector):
    inverse = lax.rsqrt(jnp.mean(row_values * row_values, axis=-1, keepdims=True) + norm_eps)
    normed = row_values * inverse
    return (normed, inverse, normed * gain_vector)


def norm_backward(grad_rows, normed, inverse, gain_vector):
    scaled = grad_rows * gain_vector
    return inverse * (scaled - normed * jnp.mean(scaled * normed, axis=-1, keepdims=True))


def adamw(weight, gradient, first_moment, second_moment, step_rate, decay_factor):
    first_new = beta_one * first_moment + (1.0 - beta_one) * gradient
    second_new = beta_two * second_moment + (1.0 - beta_two) * gradient * gradient
    first_hat = first_new / (1.0 - beta_one**STEP)
    second_hat = second_new / (1.0 - beta_two**STEP)
    weight_new = weight - step_rate * (
        first_hat / (jnp.sqrt(second_hat) + adam_eps) + decay_factor * weight
    )
    return (weight_new, first_new, second_new)


def upright(matrix):
    return with_layout_constraint(matrix, Layout(major_to_minor=(0, 1)))


def divisor_tile(extent, unit, most):
    best = extent
    for tile in range(unit, min(extent, most) + 1, unit):
        if extent % tile == 0:
            best = tile
    return best


def feed_kernel(chunks, *refs):
    m_refs, e_refs = refs[:chunks], refs[chunks : 2 * chunks]
    w_ref, d_ref = refs[2 * chunks : 2 * chunks + 2]
    v_ref, p_ref = refs[-2:]
    unit_tile = d_ref.shape[1]
    for q in range(chunks):
        both = jnp.dot(m_refs[q][...], w_ref[...], preferred_element_type=full)
        grad_act = jnp.dot(e_refs[q][0], d_ref[...], preferred_element_type=full)
        gate_pre, up_pre = both[:, :unit_tile], both[:, unit_tile:]
        sigmoid_gate = jax.nn.sigmoid(gate_pre)
        silu_gate = gate_pre * sigmoid_gate
        v_ref[q, 0] = (silu_gate * up_pre).astype(half)
        p_ref[q, 0, :, :unit_tile] = (
            grad_act * up_pre * sigmoid_gate * (1.0 + gate_pre * (1.0 - sigmoid_gate))
        ).astype(half)
        p_ref[q, 0, :, unit_tile:] = (grad_act * silu_gate).astype(half)


def feed_core(m_chunks, e_parts, feed_full, unit_tile, side, held):
    chunks = len(m_chunks)
    count, width = m_chunks[0].shape
    units = feed_full.shape[1] // 3
    steps = units // unit_tile
    down, down_base = feed_full, 2 * steps
    if unit_tile % 128:
        down, down_base = feed_full[:, 2 * units :], 0
    chunk_spec = pl.BlockSpec((count, width), lambda j: (0, 0))

    def row_spec(columns):
        return pl.BlockSpec((chunks, 1, count, columns), lambda j: (0, side, 0, j))

    held_rows = e_parts[0].shape[0]
    e_places = [divmod(2 * q + side, held_rows) for q in range(chunks)]
    operands = list(m_chunks) + [e_parts[part] for part, _ in e_places] + [feed_full, down]
    in_specs = [chunk_spec] * chunks
    in_specs += [
        pl.BlockSpec((1, count, width), lambda j, row=row: (row, 0, 0)) for _, row in e_places
    ]
    in_specs += [
        pl.BlockSpec((width, 2 * unit_tile), lambda j: (0, j)),
        pl.BlockSpec((width, unit_tile), lambda j: (0, down_base + j)),
    ]
    aliases = {}
    if held is not None:
        aliases = {len(operands) + i: i for i in range(2)}
        operands += list(held)
        in_specs += [pl.BlockSpec(memory_space=pl.ANY)] * 2
    work = chunks * count
    return pl.pallas_call(
        functools.partial(feed_kernel, chunks),
        out_shape=tuple(
            jax.ShapeDtypeStruct((chunks, 2, count, c), half) for c in (units, 2 * units)
        ),
        grid=(steps,),
        in_specs=in_specs,
        out_specs=(row_spec(unit_tile), row_spec(2 * unit_tile)),
        input_output_aliases=aliases,
        cost_estimate=pl.CostEstimate(
            flops=6 * work * width * units,
            bytes_accessed=4 * work * width + 6 * width * units + 6 * work * units,
            transcendentals=work * units,
        ),
        compiler_params=pltpu.CompilerParams(vmem_limit_bytes=56 << 20),
        name="feed_core",
    )(*operands)


def interleave(gate, up, tile):
    pieces = []
    for start in range(0, gate.shape[1], tile):
        pieces += [gate[:, start : start + tile], up[:, start : start + tile]]
    return pieces


def separate(both, tile):
    pieces = [both[:, start : start + tile] for start in range(0, both.shape[1], tile)]
    return jnp.concatenate(pieces[::2], axis=1), jnp.concatenate(pieces[1::2], axis=1)


def on_device(*arguments):
    hidden, out_cotangent = arguments[:2]
    weights, firsts, seconds = (arguments[2 + 8 * i : 10 + 8 * i] for i in range(3))
    (
        mixer_gain,
        input_weight,
        conv_weight,
        output_weight,
        feed_gain,
        gate_weight,
        up_weight,
        down_weight,
    ) = weights
    parts = lax.axis_size("tensor")
    place = lax.axis_index("tensor")
    seqs, rows, width = hidden.shape
    channels = input_weight.shape[2]
    units = gate_weight.shape[1]

    mixer_own = jnp.concatenate(
        [input_weight[:, k].astype(half) for k in range(3)] + [output_weight.T.astype(half)],
        axis=1,
    )
    unit_tile = divisor_tile(units, 128, 384)
    feed_own = jnp.concatenate(
        interleave(gate_weight.astype(half), up_weight.astype(half), unit_tile)
        + [down_weight.T.astype(half)],
        axis=1,
    )
    ring = ring_of()
    hops = ring_hops(mixer_own, ring)
    mixer_full = ring_place(mixer_own, hops, ring)
    input_full = mixer_full[:, : 3 * channels]
    output_full = mixer_full[:, 3 * channels :]

    feed_full = ring_place(feed_own, ring_hops(feed_own, ring), ring)

    channel_start = place * channels
    taps = lax.dynamic_slice_in_dim(conv_weight, channel_start, channels, 1)
    normed_one, inverse_one, scaled_one = norm_forward(hidden, mixer_gain)
    first_half, last_hop = (hops[min(1, len(hops) - 1)], hops[-1]) if hops else ((None,), (None,))
    gathered = {}

    def ring_first(arrived):
        gathered["a"] = arrived
        return tuple(h for h in first_half if h is not None)

    def mixer_first(arrived):
        gathered["e"] = arrived
        return tuple(h for h in last_hop if h is not None)

    mixer_rows = gather_rows(scaled_one.astype(half), ring_first)
    out_parts = [
        part.reshape(part.shape[0], seqs * rows, width)
        for part in gather_rows(
            after(out_cotangent.astype(half), *([gathered["a"]] if gathered else [])),
            mixer_first,
            joined=False,
        )
        if part is not None
    ]
    projected = jnp.einsum("kstd,de->kste", mixer_rows, input_full, preferred_element_type=full)
    part_b = projected[..., :channels]
    part_c = projected[..., channels : 2 * channels]
    part_x = projected[..., 2 * channels :]
    gated_in = (part_b * part_x).astype(half)

    places = [place ^ reversed_bits(p, parts) for p in range(parts)]

    def pick(pieces, wanted):
        chosen = jnp.zeros_like(pieces[0])
        for k in range(parts):
            chosen = jnp.where(places[k] == wanted, pieces[k], chosen)
        return chosen

    tails = [gated_in[k, :, rows - 2 :] for k in range(parts)]
    carried = shifted(pick(tails, parts - 1), "seq", 1)
    before = jnp.stack(
        [
            jnp.where(places[k] == 0, carried, pick(tails, places[k] - 1))
            for k in range(parts)
        ]
    )
    padded = jnp.concatenate((before, gated_in), axis=2).astype(full)
    conv_out = (
        taps[0] * padded[:, :, :rows]
        + taps[1] * padded[:, :, 1 : rows + 1]
        + taps[2] * padded[:, :, 2:]
    )
    mixed_out = (part_c * conv_out).astype(half)
    if "e" in gathered:
        mixed_out = after(mixed_out, gathered["e"])

    def narrow(pattern, left, right):
        return jnp.einsum(pattern, left, right, preferred_element_type=full)

    branch = reduce_rows(
        lambda low, high: narrow("kstc,dc->kstd", mixed_out[low:high], output_full)
    )
    middle = hidden + branch

    normed_two, inverse_two, scaled_two = norm_forward(middle, feed_gain)
    chunk_rows = seqs * rows
    feed_sent = after(scaled_two.astype(half), *out_parts)
    feed_chunks = gather_chunks(feed_sent.reshape(chunk_rows, width))
    held = None
    for side in range(2):
        held = feed_core(feed_chunks[side::2], out_parts, feed_full, unit_tile, side, held)
    activated, grad_pre = (h.reshape((parts, chunk_rows, h.shape[-1])) for h in held)
    gate_up_full = feed_full[:, : 2 * units]
    down_full = feed_full[:, 2 * units :]

    def feed_back(low, high):
        return narrow("ktf,df->ktd", grad_pre[low:high], gate_up_full)

    grads = {}

    def weight_grads(sent, near):
        left = jnp.stack([after(c, sent, near) for c in feed_chunks])
        right = jnp.concatenate([after(p, sent, near) for p in out_parts])
        grads["gate_up"] = upright(narrow("ktd,ktf->df", left, grad_pre).astype(half))
        grads["down"] = upright(narrow("ktd,ktf->df", right, activated).astype(half))
        return (grads["gate_up"], grads["down"])

    grad_scaled_two = reduce_rows(feed_back, 2, weight_grads).reshape(seqs, rows, width)
    if not grads:
        weight_grads(grad_scaled_two, grad_scaled_two)
    feed_gain_part = jnp.sum(grad_scaled_two * normed_two, axis=(0, 1))
    grad_middle = out_cotangent + norm_backward(
        grad_scaled_two, normed_two, inverse_two, feed_gain
    )
    middle_sent = grad_middle.astype(half)
    sums = {}

    def feed_output(arrived):
        held_back = after(activated, grads["gate_up"], grads["down"], middle_sent)
        sums["f"] = reduce_rows(
            lambda low, high: narrow("ktf,df->ktd", held_back[low:high], down_full),
            hold=(arrived,),
            notes=sums,
        )
        return tuple(sums[key] for key in ("sent", "near") if key in sums)

    middle_rows = gather_rows(middle_sent, feed_output)
    if not sums:
        feed_output(middle_sent)
    block_output = middle + sums["f"].reshape(seqs, rows, width)

    grad_mixed = narrow("kstd,dc->kstc", middle_rows, output_full)
    grad_output = narrow("kstd,kstc->dc", middle_rows, mixed_out).astype(half)
    grad_c = grad_mixed * conv_out
    grad_conv_out = grad_mixed * part_c
    conv_part = jnp.stack(
        [
            jnp.sum(grad_conv_out * padded[:, :, tap : tap + rows], axis=(0, 1, 2))
            for tap in range(3)
        ]
    )
    heads = [grad_conv_out[k, :, :2] for k in range(parts)]
    owned_feed = upright(ring_scatter((grads["gate_up"], grads["down"]), (), ((), (), heads)))
    owned_gate_up, owned_down = owned_feed[:, : 2 * units], upright(owned_feed[:, 2 * units :].T)
    following = after(shifted(pick(heads, 0), "seq", -1), grad_output)
    following_rows = jnp.stack(
        [
            jnp.where(places[k] == parts - 1, following, pick(heads, places[k] + 1))
            for k in range(parts)
        ]
    )
    conv_tail = jnp.concatenate((grad_conv_out, following_rows), axis=2)
    grad_gated = (
        taps[0] * conv_tail[:, :, 2:]
        + taps[1] * conv_tail[:, :, 1 : rows + 1]
        + taps[2] * conv_tail[:, :, :rows]
    )
    grad_projected = jnp.concatenate(
        (
            (grad_gated * part_x).astype(half),
            grad_c.astype(half),
            (grad_gated * part_b).astype(half),
        ),
        axis=-1,
    )
    if "arrived" in sums:
        grad_projected = after(grad_projected, sums["arrived"])
    grad_input = narrow("kstd,kste->de", mixer_rows, grad_projected).astype(half)
    (grad_input,) = lax.optimization_barrier((upright(grad_input),))
    mixer_gain_part = (
        jnp.sum(grad_input.astype(full) * input_full.astype(full), axis=1)
        / mixer_gain
    )
    conv_placed = lax.dynamic_update_slice_in_dim(
        jnp.zeros(conv_weight.shape, full), conv_part, channel_start, 1
    )
    vectors = sum_everywhere(
        jnp.concatenate((mixer_gain_part[None], feed_gain_part[None], conv_placed), axis=0)
    )
    steps = {}

    def back_product(low, high):
        steps[low] = narrow("kste,de->kstd", grad_projected[low:high], input_full)
        return steps[low]

    grad_scaled_one = reduce_rows(back_product, notes=steps)
    far = [steps["sent"], steps["near"]] if "sent" in steps else []
    owned_mixer = upright(ring_scatter((grad_input, upright(grad_output)), ((), far)))
    hidden_grad = grad_middle + norm_backward(
        grad_scaled_one, normed_one, inverse_one, mixer_gain
    )

    owned_gate, owned_up = separate(owned_gate_up, unit_tile)
    gradients = (
        vectors[0],
        jnp.stack(
            [owned_mixer[:, k * channels : (k + 1) * channels] for k in range(3)], axis=1
        ),
        vectors[2:],
        upright(owned_mixer[:, 3 * channels :].T),
        vectors[1],
        owned_gate,
        owned_up,
        owned_down,
    )
    vector_flags = (True, False, True, False, True, False, False, False)
    updated = [
        adamw(
            weight,
            gradient,
            first,
            second,
            vector_rate if flag else matrix_rate,
            0.0 if flag else decay_rate,
        )
        for weight, gradient, first, second, flag in zip(
            weights, gradients, firsts, seconds, vector_flags
        )
    ]
    return (
        (block_output, hidden_grad)
        + gradients
        + tuple(u[0] for u in updated)
        + tuple(u[1] for u in updated)
        + tuple(u[2] for u in updated)
    )


def solution(mesh):
    row_spec = P("dp", ("seq", "tensor"), None)
    weight_specs = (
        P(),
        P(owners, None, "tensor"),
        P(),
        P("tensor", owners),
        P(),
        P(owners, "tensor"),
        P(owners, "tensor"),
        P("tensor", owners),
    )
    in_specs = (row_spec, row_spec) + weight_specs * 3
    out_specs = (row_spec, row_spec) + weight_specs * 4
    return jax.shard_map(
        on_device, mesh=mesh, in_specs=in_specs, out_specs=out_specs, check_vma=False
    )
```

```python
import functools

import jax
import jax.numpy as jnp
from jax import lax
from jax.experimental import pallas as pl
from jax.experimental.layout import Layout, with_layout_constraint
from jax.experimental.pallas import tpu as pltpu
from jax.sharding import PartitionSpec as P


STEP = 3

norm_eps = 1e-05
beta_one = 0.9
beta_two = 0.95
adam_eps = 1e-08
matrix_rate = 0.005
vector_rate = 0.05
decay_rate = 0.1

half = jnp.bfloat16
full = jnp.float32
owners = ("dp", "seq")


def shifted(block, axis, distance):
    devices = range(lax.axis_size(axis))
    route = [(i - distance, i) for i in devices if i - distance in devices]
    return lax.ppermute(block, axis, route)


def swapped(block, axis, distance):
    return lax.ppermute(block, axis, [(i, i ^ distance) for i in range(lax.axis_size(axis))])


def after(value, *others):
    return lax.optimization_barrier((value,) + others)[0]


def bits_of(size):
    return [1 << b for b in range(size.bit_length() - 1)]


def reversed_bits(index, size):
    return int(f"{index + size:b}"[:0:-1], 2) if size > 1 else 0


def gather_rows(block, between=None, joined=True):
    stack, arrived = block[None], None
    for distance in reversed(bits_of(lax.axis_size("tensor"))):
        if arrived is not None:
            stack = jnp.concatenate((stack, arrived))
        arrived = swapped(stack, "tensor", distance)
        if between is not None:
            arrived = after(arrived, *between(arrived))
            between = None
    if not joined:
        return stack, arrived
    return stack if arrived is None else jnp.concatenate((stack, arrived))


def gather_chunks(block):
    size = lax.axis_size("tensor")
    chunks = {0: block}
    for distance in reversed(bits_of(size)):
        for k in sorted(chunks):
            chunks[k ^ distance] = swapped(chunks[k], "tensor", distance)
    return [chunks[reversed_bits(p, size)] for p in range(size)]


def reduce_rows(partial_of, pieces=1, between=None, hold=(), notes=None):
    size = lax.axis_size("tensor")
    if size == 1:
        return partial_of(0, 1)[0]
    low = size // 2
    step = low // pieces
    arrived = {}
    for start in reversed(range(low, size, step)):
        sent = partial_of(start, start + step).astype(half)
        arrived[start - low] = swapped(sent, "tensor", 1).astype(full)
    sums = {}
    quarter = max(low // 2, 1)
    for start in reversed(range(0, low, quarter)):
        if step >= quarter:
            key = start - start % step
            piece = arrived[key][start - key : start - key + quarter]
        else:
            piece = jnp.concatenate([arrived[k] for k in range(start, start + quarter, step)])
        sums[start] = partial_of(start, start + quarter) + piece
    if low == 1:
        return sums[0][0]
    far, near = sums[quarter], sums[0]
    distance = 2
    while True:
        sent = far.astype(half)
        (near,) = lax.optimization_barrier((near,))
        if notes is not None:
            notes["sent"], notes["near"] = sent, near
        if hold:
            sent = after(sent, *hold)
            hold = ()
        arrived = swapped(sent, "tensor", distance)
        if notes is not None:
            notes["arrived"] = arrived
            notes = None
        if between is not None:
            arrived = after(arrived, *between(sent, near))
            between = None
        near = near + arrived.astype(full)
        if near.shape[0] == 1:
            return near[0]
        distance *= 2
        middle = near.shape[0] // 2
        far, near = near[middle:], near[:middle]


def ring_of():
    rows, columns = lax.axis_size("dp"), lax.axis_size("seq")
    ring = []
    for r in range(rows):
        line = [r * columns + c for c in range(columns)]
        ring += line if r % 2 == 0 else line[::-1]
    return ring


def folded(row, column, columns):
    return row * columns + jnp.where(row % 2 == 1, columns - 1 - column, column)


def ring_neighbour(ring, offset):
    size, columns = len(ring), lax.axis_size("seq")
    own = folded(lax.axis_index("dp"), lax.axis_index("seq"), columns)
    target = lax.rem(own + (offset + size), size)
    return folded(lax.div(target, columns), lax.rem(target, columns), columns)


def ring_shift(block, ring, direction):
    size = len(ring)
    return lax.ppermute(
        block, owners, [(ring[p], ring[(p + direction) % size]) for p in range(size)]
    )


def ring_hops(block, ring):
    size = len(ring)
    forward = backward = block
    hops = []
    for hop in range(1, size // 2 + 1):
        forward = ring_shift(forward, ring, 1)
        backward = ring_shift(backward, ring, -1) if hop <= (size - 1) // 2 else None
        hops.append((forward, backward))
    return hops


def ring_place(block, hops, ring):
    rows = block.shape[0]
    result = jnp.zeros((rows * len(ring),) + block.shape[1:], block.dtype)
    pieces = [(0, block)]
    for hop, (forward, backward) in enumerate(hops, 1):
        pieces.append((-hop, forward))
        if backward is not None:
            pieces.append((hop, backward))
    for offset, piece in pieces:
        start = ring_neighbour(ring, offset) * rows
        result = lax.dynamic_update_slice_in_dim(result, piece, start, 0)
    return result


def ring_scatter(partials, holds=(), reads=(), notes=None):
    ring = ring_of()
    size = len(ring)
    rows = partials[0].shape[0] // size

    def piece(offset):
        start = ring_neighbour(ring, offset) * rows
        return jnp.concatenate(
            [lax.dynamic_slice_in_dim(p, start, rows, 0) for p in partials], axis=1
        ).astype(full)

    total = piece(0)
    running = {1: None, -1: None}
    for step in range(size // 2):
        for direction, reach in ((1, size // 2), (-1, (size - 1) // 2)):
            hop = reach - step
            if hop <= 0:
                continue
            own = piece(direction * hop)
            if running[direction] is not None:
                addend = running[direction]
                if step < len(reads) and reads[step]:
                    addend = after(addend, *reads[step])
                own = own + addend.astype(full)
            sent = own.astype(half)
            if step < len(holds) and holds[step]:
                sent = after(sent, *holds[step])
            if notes is not None:
                notes.setdefault(step, []).append(sent)
            running[direction] = ring_shift(sent, ring, direction)
    for arrived in running.values():
        if arrived is not None:
            total = total + arrived.astype(full)
    return total


def sum_everywhere(block, reads=()):
    hops = [(axis, d) for axis in ("tensor", "dp", "seq") for d in bits_of(lax.axis_size(axis))]
    hops.sort(key=lambda hop: hop[0] == "tensor" and hop[1] > 1)
    for step, (axis, distance) in enumerate(hops):
        arrived = swapped(block, axis, distance)
        if step + 1 < len(reads) and reads[step + 1]:
            arrived = after(arrived, *reads[step + 1])
        block = block + arrived
    return block


def norm_forward(row_values, gain_vector):
    inverse = lax.rsqrt(jnp.mean(row_values * row_values, axis=-1, keepdims=True) + norm_eps)
    normed = row_values * inverse
    return (normed, inverse, normed * gain_vector)


def norm_backward(grad_rows, normed, inverse, gain_vector):
    scaled = grad_rows * gain_vector
    return inverse * (scaled - normed * jnp.mean(scaled * normed, axis=-1, keepdims=True))


def adamw(weight, gradient, first_moment, second_moment, step_rate, decay_factor):
    first_new = beta_one * first_moment + (1.0 - beta_one) * gradient
    second_new = beta_two * second_moment + (1.0 - beta_two) * gradient * gradient
    first_hat = first_new / (1.0 - beta_one**STEP)
    second_hat = second_new / (1.0 - beta_two**STEP)
    weight_new = weight - step_rate * (
        first_hat / (jnp.sqrt(second_hat) + adam_eps) + decay_factor * weight
    )
    return (weight_new, first_new, second_new)


def upright(matrix):
    return with_layout_constraint(matrix, Layout(major_to_minor=(0, 1)))


def divisor_tile(extent, unit, most):
    best = extent
    for tile in range(unit, min(extent, most) + 1, unit):
        if extent % tile == 0:
            best = tile
    return best


def feed_kernel(chunks, *refs):
    m_refs, e_refs = refs[:chunks], refs[chunks : 2 * chunks]
    w_ref, d_ref = refs[2 * chunks : 2 * chunks + 2]
    v_ref, p_ref = refs[-2:]
    unit_tile = d_ref.shape[1]
    for q in range(chunks):
        both = jnp.dot(m_refs[q][...], w_ref[...], preferred_element_type=full)
        grad_act = jnp.dot(e_refs[q][0], d_ref[...], preferred_element_type=full)
        gate_pre, up_pre = both[:, :unit_tile], both[:, unit_tile:]
        sigmoid_gate = jax.nn.sigmoid(gate_pre)
        silu_gate = gate_pre * sigmoid_gate
        v_ref[q, 0] = (silu_gate * up_pre).astype(half)
        p_ref[q, 0, :, :unit_tile] = (
            grad_act * up_pre * sigmoid_gate * (1.0 + gate_pre * (1.0 - sigmoid_gate))
        ).astype(half)
        p_ref[q, 0, :, unit_tile:] = (grad_act * silu_gate).astype(half)


def feed_core(m_chunks, e_parts, feed_full, unit_tile, side, held):
    chunks = len(m_chunks)
    count, width = m_chunks[0].shape
    units = feed_full.shape[1] // 3
    steps = units // unit_tile
    down, down_base = feed_full, 2 * steps
    if unit_tile % 128:
        down, down_base = feed_full[:, 2 * units :], 0
    chunk_spec = pl.BlockSpec((count, width), lambda j: (0, 0))

    def row_spec(columns):
        return pl.BlockSpec((chunks, 1, count, columns), lambda j: (0, side, 0, j))

    held_rows = e_parts[0].shape[0]
    e_places = [divmod(2 * q + side, held_rows) for q in range(chunks)]
    operands = list(m_chunks) + [e_parts[part] for part, _ in e_places] + [feed_full, down]
    in_specs = [chunk_spec] * chunks
    in_specs += [
        pl.BlockSpec((1, count, width), lambda j, row=row: (row, 0, 0)) for _, row in e_places
    ]
    in_specs += [
        pl.BlockSpec((width, 2 * unit_tile), lambda j: (0, j)),
        pl.BlockSpec((width, unit_tile), lambda j: (0, down_base + j)),
    ]
    aliases = {}
    if held is not None:
        aliases = {len(operands) + i: i for i in range(2)}
        operands += list(held)
        in_specs += [pl.BlockSpec(memory_space=pl.ANY)] * 2
    work = chunks * count
    return pl.pallas_call(
        functools.partial(feed_kernel, chunks),
        out_shape=tuple(
            jax.ShapeDtypeStruct((chunks, 2, count, c), half) for c in (units, 2 * units)
        ),
        grid=(steps,),
        in_specs=in_specs,
        out_specs=(row_spec(unit_tile), row_spec(2 * unit_tile)),
        input_output_aliases=aliases,
        cost_estimate=pl.CostEstimate(
            flops=6 * work * width * units,
            bytes_accessed=4 * work * width + 6 * width * units + 6 * work * units,
            transcendentals=work * units,
        ),
        compiler_params=pltpu.CompilerParams(vmem_limit_bytes=56 << 20),
        name="feed_core",
    )(*operands)


def interleave(gate, up, tile):
    pieces = []
    for start in range(0, gate.shape[1], tile):
        pieces += [gate[:, start : start + tile], up[:, start : start + tile]]
    return pieces


def separate(both, tile):
    pieces = [both[:, start : start + tile] for start in range(0, both.shape[1], tile)]
    return jnp.concatenate(pieces[::2], axis=1), jnp.concatenate(pieces[1::2], axis=1)


def on_device(*arguments):
    hidden, out_cotangent = arguments[:2]
    weights, firsts, seconds = (arguments[2 + 8 * i : 10 + 8 * i] for i in range(3))
    (
        mixer_gain,
        input_weight,
        conv_weight,
        output_weight,
        feed_gain,
        gate_weight,
        up_weight,
        down_weight,
    ) = weights
    parts = lax.axis_size("tensor")
    place = lax.axis_index("tensor")
    seqs, rows, width = hidden.shape
    channels = input_weight.shape[2]
    units = gate_weight.shape[1]

    mixer_own = jnp.concatenate(
        [input_weight[:, k].astype(half) for k in range(3)] + [output_weight.T.astype(half)],
        axis=1,
    )
    unit_tile = divisor_tile(units, 128, 384)
    feed_own = jnp.concatenate(
        interleave(gate_weight.astype(half), up_weight.astype(half), unit_tile)
        + [down_weight.T.astype(half)],
        axis=1,
    )
    ring = ring_of()
    hops = ring_hops(mixer_own, ring)
    mixer_full = ring_place(mixer_own, hops, ring)
    input_full = mixer_full[:, : 3 * channels]
    output_full = mixer_full[:, 3 * channels :]

    feed_full = ring_place(feed_own, ring_hops(feed_own, ring), ring)

    channel_start = place * channels
    taps = lax.dynamic_slice_in_dim(conv_weight, channel_start, channels, 1)
    normed_one, inverse_one, scaled_one = norm_forward(hidden, mixer_gain)
    first_half, last_hop = (hops[min(1, len(hops) - 1)], hops[-1]) if hops else ((None,), (None,))
    gathered = {}

    def ring_first(arrived):
        gathered["a"] = arrived
        return tuple(h for h in first_half if h is not None)

    def mixer_first(arrived):
        gathered["e"] = arrived
        return tuple(h for h in last_hop if h is not None)

    mixer_rows = gather_rows(scaled_one.astype(half), ring_first)
    out_parts = [
        part.reshape(part.shape[0], seqs * rows, width)
        for part in gather_rows(
            after(out_cotangent.astype(half), *([gathered["a"]] if gathered else [])),
            mixer_first,
            joined=False,
        )
        if part is not None
    ]
    projected = jnp.einsum("kstd,de->kste", mixer_rows, input_full, preferred_element_type=full)
    part_b = projected[..., :channels]
    part_c = projected[..., channels : 2 * channels]
    part_x = projected[..., 2 * channels :]
    gated_in = (part_b * part_x).astype(half)

    places = [place ^ reversed_bits(p, parts) for p in range(parts)]

    def pick(pieces, wanted):
        chosen = jnp.zeros_like(pieces[0])
        for k in range(parts):
            chosen = jnp.where(places[k] == wanted, pieces[k], chosen)
        return chosen

    tails = [gated_in[k, :, rows - 2 :] for k in range(parts)]
    carried = shifted(pick(tails, parts - 1), "seq", 1)
    before = jnp.stack(
        [
            jnp.where(places[k] == 0, carried, pick(tails, places[k] - 1))
            for k in range(parts)
        ]
    )
    padded = jnp.concatenate((before, gated_in), axis=2).astype(full)
    conv_out = (
        taps[0] * padded[:, :, :rows]
        + taps[1] * padded[:, :, 1 : rows + 1]
        + taps[2] * padded[:, :, 2:]
    )
    mixed_out = (part_c * conv_out).astype(half)
    if "e" in gathered:
        mixed_out = after(mixed_out, gathered["e"])

    def narrow(pattern, left, right):
        return jnp.einsum(pattern, left, right, preferred_element_type=full)

    branch = reduce_rows(
        lambda low, high: narrow("kstc,dc->kstd", mixed_out[low:high], output_full)
    )
    middle = hidden + branch

    normed_two, inverse_two, scaled_two = norm_forward(middle, feed_gain)
    chunk_rows = seqs * rows
    feed_sent = after(scaled_two.astype(half), *out_parts)
    feed_chunks = gather_chunks(feed_sent.reshape(chunk_rows, width))
    held = None
    for side in range(2):
        held = feed_core(feed_chunks[side::2], out_parts, feed_full, unit_tile, side, held)
    activated, grad_pre = (h.reshape((parts, chunk_rows, h.shape[-1])) for h in held)
    gate_up_full = feed_full[:, : 2 * units]
    down_full = feed_full[:, 2 * units :]

    def feed_back(low, high):
        return narrow("ktf,df->ktd", grad_pre[low:high], gate_up_full)

    grads = {}

    def weight_grads(sent, near):
        left = jnp.stack([after(c, sent, near) for c in feed_chunks])
        right = jnp.concatenate([after(p, sent, near) for p in out_parts])
        grads["gate_up"] = upright(narrow("ktd,ktf->df", left, grad_pre).astype(half))
        grads["down"] = upright(narrow("ktd,ktf->df", right, activated).astype(half))
        return (grads["gate_up"], grads["down"])

    grad_scaled_two = reduce_rows(feed_back, 2, weight_grads).reshape(seqs, rows, width)
    if not grads:
        weight_grads(grad_scaled_two, grad_scaled_two)
    feed_gain_part = jnp.sum(grad_scaled_two * normed_two, axis=(0, 1))
    grad_middle = out_cotangent + norm_backward(
        grad_scaled_two, normed_two, inverse_two, feed_gain
    )
    middle_sent = grad_middle.astype(half)
    sums = {}

    def feed_output(arrived):
        held_back = after(activated, grads["gate_up"], grads["down"], middle_sent)
        sums["f"] = reduce_rows(
            lambda low, high: narrow("ktf,df->ktd", held_back[low:high], down_full),
            hold=(arrived,),
            notes=sums,
        )
        return tuple(sums[key] for key in ("sent", "near") if key in sums)

    middle_rows = gather_rows(middle_sent, feed_output)
    if not sums:
        feed_output(middle_sent)
    block_output = middle + sums["f"].reshape(seqs, rows, width)

    grad_mixed = narrow("kstd,dc->kstc", middle_rows, output_full)
    grad_output = narrow("kstd,kstc->dc", middle_rows, mixed_out).astype(half)
    grad_c = grad_mixed * conv_out
    grad_conv_out = grad_mixed * part_c
    conv_part = jnp.stack(
        [
            jnp.sum(grad_conv_out * padded[:, :, tap : tap + rows], axis=(0, 1, 2))
            for tap in range(3)
        ]
    )
    heads = [grad_conv_out[k, :, :2] for k in range(parts)]
    following = after(shifted(pick(heads, 0), "seq", -1), grad_output)
    owned_feed = upright(
        ring_scatter((grads["gate_up"], grads["down"]), (), ((), (), (following,)))
    )
    owned_gate_up, owned_down = owned_feed[:, : 2 * units], upright(owned_feed[:, 2 * units :].T)
    following_rows = jnp.stack(
        [
            jnp.where(places[k] == parts - 1, following, pick(heads, places[k] + 1))
            for k in range(parts)
        ]
    )
    conv_tail = jnp.concatenate((grad_conv_out, following_rows), axis=2)
    grad_gated = (
        taps[0] * conv_tail[:, :, 2:]
        + taps[1] * conv_tail[:, :, 1 : rows + 1]
        + taps[2] * conv_tail[:, :, :rows]
    )
    grad_projected = jnp.concatenate(
        (
            (grad_gated * part_x).astype(half),
            grad_c.astype(half),
            (grad_gated * part_b).astype(half),
        ),
        axis=-1,
    )
    grad_input = narrow("kstd,kste->de", mixer_rows, grad_projected).astype(half)
    (grad_input,) = lax.optimization_barrier((upright(grad_input),))
    mixer_gain_part = (
        jnp.sum(grad_input.astype(full) * input_full.astype(full), axis=1)
        / mixer_gain
    )
    steps = {}

    def back_product(low, high):
        steps[low] = narrow("kste,de->kstd", grad_projected[low:high], input_full)
        return steps[low]

    grad_scaled_one = reduce_rows(back_product, notes=steps)
    far = [steps["sent"], steps["near"]] if "sent" in steps else []
    ring_sent = {}
    owned_mixer = upright(
        ring_scatter((grad_input, upright(grad_output)), ((), far), (), ring_sent)
    )
    conv_placed = lax.dynamic_update_slice_in_dim(
        jnp.zeros(conv_weight.shape, full), conv_part, channel_start, 1
    )
    vectors = sum_everywhere(
        jnp.concatenate((mixer_gain_part[None], feed_gain_part[None], conv_placed), axis=0),
        ((), (), ring_sent.get(2, ()), ring_sent.get(3, ())),
    )
    hidden_grad = grad_middle + norm_backward(
        grad_scaled_one, normed_one, inverse_one, mixer_gain
    )

    owned_gate, owned_up = separate(owned_gate_up, unit_tile)
    gradients = (
        vectors[0],
        jnp.stack(
            [owned_mixer[:, k * channels : (k + 1) * channels] for k in range(3)], axis=1
        ),
        vectors[2:],
        upright(owned_mixer[:, 3 * channels :].T),
        vectors[1],
        owned_gate,
        owned_up,
        owned_down,
    )
    vector_flags = (True, False, True, False, True, False, False, False)
    updated = []
    for k, flag in enumerate(vector_flags):
        updated.append(
            adamw(
                weights[k],
                gradients[k],
                firsts[k],
                seconds[k],
                vector_rate if flag else matrix_rate,
                0.0 if flag else decay_rate,
            )
        )
    return (
        (block_output, hidden_grad)
        + gradients
        + tuple(u[0] for u in updated)
        + tuple(u[1] for u in updated)
        + tuple(u[2] for u in updated)
    )


def solution(mesh):
    row_spec = P("dp", ("seq", "tensor"), None)
    weight_specs = (
        P(),
        P(owners, None, "tensor"),
        P(),
        P("tensor", owners),
        P(),
        P(owners, "tensor"),
        P(owners, "tensor"),
        P("tensor", owners),
    )
    in_specs = (row_spec, row_spec) + weight_specs * 3
    out_specs = (row_spec, row_spec) + weight_specs * 4
    return jax.shard_map(
        on_device, mesh=mesh, in_specs=in_specs, out_specs=out_specs, check_vma=False
    )
```
